128 devices in a mesh: segment: 2 (over core), expert: 64 (over x, y, z).
Axes of the slice: x: 4, y: 4, z: 4, core: 2. Of those that a mesh axis runs over, the one named last changes fastest.
Arguments:
- tokens: bfloat16 [2, 1024, 4096], P(None, 'expert'), may hold values from -6 to 6
- expert_ids: int32 [2, 2, 1024, 8], P('segment', None, 'expert'), may hold values from 0 to 63, all different within a row; in each aligned block of 16 rows (0 to 15, 16 to 31, ..., all dimensions but the last counted through in order) at most 4 rows name the same one
- gate_weights: float32 [2, 2, 1024, 8], P('segment', None, 'expert'), may hold values from 0.05 to 0.5
- norm_gain: float32 [2, 4096], P('segment'), may hold values from 0.25 to 1.75
- w_gate: bfloat16 [2, 64, 4096, 768], P('segment', 'expert'), may hold values from -0.09375 to 0.09375
- w_up: bfloat16 [2, 64, 4096, 768], P('segment', 'expert'), may hold values from -0.09375 to 0.09375
- w_down: bfloat16 [2, 64, 768, 4096], P('segment', 'expert'), may hold values from -0.21875 to 0.21875
Outputs:
- section_out: bfloat16 [2, 2, 1024, 4096], P('segment', None, 'expert')
The draws below stay inside these ranges and needn't reach their ends.
Inputs may be any that keep to these rules, and one draw needn't show every extreme that they name: `expert_ids`: each row names 8 different experts. In each aligned block of 16 rows (the rows of one device for one section and micro-batch) no expert is named more than 4 times, a bound that some block reaches.
All inputs are finite; a program needn't handle non-finite values.
Results may differ from the reference program's by a relative error of at most 0.0059.
Values may be sent and summed in bfloat16 or wider, within the bound.
No kernel may reach another device: no remote copies, remote signals or barrier semaphores. Data moves between devices by JAX's collectives and lax.ppermute only.
A program may use at most 128 MiB of HBM per device.

```python
import math
import jax
import jax.numpy as jnp
import numpy as np
from jax import lax

D = 4096
FF = 768
TOP = 8
MICRO = 2
TOK_DEV = 16
SEGMENTS = 2
EXPERTS = 64
TOKENS = 1024
CAP = 4
N_SEGMENT = 2
N_EXPERT = 64


def block_scale(key, shape, split, least, high):
    def one(dim, blocks):
        steps = jax.random.uniform(jax.random.fold_in(jax.random.fold_in(key, 6), dim), (blocks,), jnp.float32, least / len(split), high / len(split))
        return jnp.repeat(jnp.exp(steps), shape[dim] // blocks).reshape((-1,) + (1,) * (len(shape) - dim - 1))

    factor_of = one(*split[0])
    for cut in split[1:]:
        factor_of = factor_of * one(*cut)
    return factor_of


def shared_out(own_key, own, number, rows, count, top, limit, skew):
    ranking = jax.random.permutation(own_key, count)
    crowded, usual = load_shares(count, rows * top, limit, skew, True), load_shares(count, rows * top, limit, skew, False)
    places = jnp.arange(count)

    def named(sizes, offset_by):
        used = int((sizes > 0).sum())
        fixed = max(1, used // 4)
        moved = fixed + (places - fixed + offset_by * (used - fixed)) % max(1, count - fixed)
        return jnp.zeros((count,), jnp.int32).at[ranking[jnp.where(places < fixed, places, moved)]].set(jnp.asarray(sizes, jnp.int32))

    sizes = jnp.where(number % 4 == 0, named(crowded, number // 4), named(usual, number - number // 4 - 1))
    mixed = jax.random.permutation(jax.random.fold_in(own, 3), count)
    source_of, receiver = mixed[0:count // 2 * 2:2], mixed[1:count // 2 * 2:2]
    margin = jnp.minimum(sizes[source_of] - 1, limit - sizes[receiver]) // 2
    margin = jnp.where((source_of == ranking[0]) | (receiver == ranking[0]) | (sizes[receiver] == 0), 0, jnp.maximum(margin, 0))
    moved = jax.random.randint(jax.random.fold_in(own, 4), (count // 2,), 0, 1 << 20) % (margin + 1)
    sizes = sizes.at[source_of].add(-moved).at[receiver].add(moved)
    members = jnp.searchsorted(jnp.cumsum(sizes), jnp.arange(rows * top), side="right").astype(jnp.int32)
    listing = members.reshape(top, rows).T
    listing = listing[jax.random.permutation(jax.random.fold_in(own, 1), rows)]
    offset_by = jax.random.randint(jax.random.fold_in(own, 2), (rows, 1), 0, top)
    return jnp.take_along_axis(listing, (jnp.arange(top)[None, :] + offset_by) % top, axis=1)


def load_shares(count, total, reach, skew, full):
    loads = [(1 << 20) // math.isqrt(grade ** skew) + 1 for grade in range(1, count + 1)]
    largest = reach if full else min(reach, max(-(-total // count), total * loads[0] // sum(loads)))
    least = 1 if total - largest >= count - 1 else 0
    counts, surplus = [largest] + [least] * (count - 1), total - largest - least * (count - 1)
    while surplus > 0:
        movable = [i for i in range(1, count) if counts[i] < largest] or [i for i in range(1, count) if counts[i] < reach]
        mass, left = sum([loads[i] for i in movable]), surplus
        for i in movable:
            addition = min(reach - counts[i], max(1, left * loads[i] // mass), surplus)
            counts[i] = counts[i] + addition
            surplus = surplus - addition
    return np.array(counts)


def normal_values(own_key, extent, scale, bound, pieces=(), kind=jnp.bfloat16):
    level = block_scale(own_key, extent, pieces, -0.22, 0.18) if pieces else 1.0
    values = jax.random.normal(own_key, extent, jnp.float32) * scale * level
    return jnp.minimum(jnp.maximum(values, -bound), bound).astype(kind)


def setup_inputs(seed: int = 0) -> dict:
    streams_of = jax.random.split(jax.random.key(seed), 8)
    tokens = normal_values(streams_of[0], (MICRO, TOKENS, D), 1.0, 6.0, ((1, 64),))
    expert_ids_keys = jax.random.split(jax.random.fold_in(streams_of[1], 1), SEGMENTS * MICRO * TOKENS // TOK_DEV)
    expert_ids_turns = jax.random.permutation(jax.random.fold_in(streams_of[1], 3), SEGMENTS * MICRO * TOKENS // TOK_DEV)
    expert_ids = jax.vmap(lambda own, number: shared_out(jax.random.fold_in(streams_of[1], 2), own, number, TOK_DEV, EXPERTS, TOP, CAP, 2))(expert_ids_keys, expert_ids_turns).reshape((SEGMENTS, MICRO, TOKENS, TOP))
    gate_weights = jnp.clip(jnp.exp(math.log(0.5) - 2.3025851 * jax.random.uniform(streams_of[2], (SEGMENTS, MICRO, TOKENS, TOP), jnp.float32) ** block_scale(streams_of[2], (SEGMENTS, MICRO, TOKENS, TOP), ((0, 2), (2, 64)), -0.2, 0.2)), 0.05, 0.5)
    norm_gain = jnp.clip(1.0 + 0.15 * jax.random.normal(streams_of[3], (SEGMENTS, D), jnp.float32), 0.25, 1.75)
    w_gate = normal_values(streams_of[4], (SEGMENTS, EXPERTS, D, FF), D ** -0.5, 0.09375, ((0, 2), (1, 64)))
    w_up = normal_values(streams_of[5], (SEGMENTS, EXPERTS, D, FF), D ** -0.5, 0.09375, ((0, 2), (1, 64)))
    w_down = normal_values(streams_of[6], (SEGMENTS, EXPERTS, FF, D), FF ** -0.5, 0.21875, ((0, 2), (1, 64)))
    return {"tokens": tokens, "expert_ids": expert_ids, "gate_weights": gate_weights, "norm_gain": norm_gain, "w_gate": w_gate, "w_up": w_up, "w_down": w_down}


def norm_rows(current, gain):
    values = current.astype(jnp.float32)
    scaled = values * lax.rsqrt(lax.optimization_barrier(jnp.mean(values * values, axis=-1, keepdims=True)) + 1e-06)
    return (scaled * gain.astype(jnp.float32)).astype(jnp.bfloat16)

def expert_apply(operands):
    row_block, gate_mat, up_mat, down_mat = operands
    gate_part = jnp.dot(row_block, gate_mat, preferred_element_type=jnp.float32)
    up_part = jnp.dot(row_block, up_mat, preferred_element_type=jnp.float32)
    hidden = (jax.nn.silu(gate_part) * up_part).astype(jnp.bfloat16)
    return jnp.dot(hidden, down_mat, preferred_element_type=jnp.float32).astype(jnp.bfloat16)

def one_layer(current, routes, weighting, gain, gate_all, up_all, down_all):
    normed = norm_rows(current, gain)
    blocks = routes.reshape(N_EXPERT, TOK_DEV * TOP).astype(jnp.int32)
    onehot = (blocks[:, :, None] == jnp.arange(EXPERTS, dtype=jnp.int32)[None, None, :]).astype(jnp.int32)
    ranks = lax.optimization_barrier(jnp.sum(jnp.cumsum(onehot, axis=1) * onehot, axis=2)) - 1
    source = jnp.arange(N_EXPERT, dtype=jnp.int32)[:, None]
    index = ((blocks * N_EXPERT + source) * CAP + ranks).reshape(-1).astype(jnp.int32)
    spread = jnp.repeat(normed, TOP, axis=0)
    dispatch_rows = jnp.zeros((EXPERTS * N_EXPERT * CAP, D), jnp.bfloat16).at[index].set(spread)
    served = lax.map(expert_apply, (dispatch_rows.reshape(EXPERTS, N_EXPERT * CAP, D), gate_all, up_all, down_all))
    picked = served.reshape(-1, D)[index].reshape(TOKENS, TOP, D)
    mixed = current.astype(jnp.float32) + lax.optimization_barrier(jnp.sum(weighting[:, :, None].astype(jnp.float32) * picked.astype(jnp.float32), axis=1))
    return mixed.astype(jnp.bfloat16)

def reference(tokens, expert_ids, gate_weights, norm_gain, w_gate, w_up, w_down):
    inputs = [tokens[micro_no] for micro_no in range(MICRO)]
    segment_outs = []
    for segment_no in range(N_SEGMENT):
        layer_outs = []
        for micro_no in range(MICRO):
            layer_outs.append(one_layer(inputs[micro_no], expert_ids[segment_no, micro_no], gate_weights[segment_no, micro_no], norm_gain[segment_no], w_gate[segment_no], w_up[segment_no], w_down[segment_no]))
        segment_outs.append(jnp.stack(layer_outs))
        inputs = layer_outs
    return jnp.stack(segment_outs)
```

```python
import functools

import jax
import jax.numpy as jnp
from jax import lax
from jax.experimental import pallas as pl
from jax.experimental.pallas import tpu as pltpu
from jax.sharding import PartitionSpec as P

VMEM = pltpu.MemorySpace.VMEM
SMEM = pltpu.MemorySpace.SMEM
SWAP = [(0, 1), (1, 0)]


def params(mib=40):
    return pltpu.CompilerParams(vmem_limit_bytes=mib << 20)


def cost(flops, moved):
    return pl.CostEstimate(flops=flops, bytes_accessed=moved, transcendentals=0)


def dispatch_body(cap, micro, core_ref, own_ref, other_ref, gain_ref, meta_ref, send_ref, comb_ref):
    rows, half = own_ref.shape
    slots = send_ref.shape[0]
    top = meta_ref.shape[1] // 2
    tok = rows // micro
    core = core_ref[0]
    lane = lax.broadcasted_iota(jnp.int32, (rows, slots), 1)
    row = lax.broadcasted_iota(jnp.int32, (rows, slots), 0)
    expert = lax.div(lane, cap * micro).astype(jnp.float32)
    rank_of = lax.rem(lane, cap).astype(jnp.float32)
    same = lax.rem(lax.div(lane, cap), micro) == lax.div(row, tok)
    named = jnp.zeros((rows, slots), jnp.float32)
    weight = jnp.zeros((rows, slots), jnp.float32)
    meta = meta_ref[...]
    for k in range(top):
        hit = meta[:, k : k + 1] == expert
        named += jnp.where(hit, 1.0, 0.0)
        weight += jnp.where(hit, meta[:, top + k : top + k + 1], 0.0)
    a = lax.broadcasted_iota(jnp.int32, (rows, rows), 0)
    b = lax.broadcasted_iota(jnp.int32, (rows, rows), 1)
    before = jnp.where((b < a) & (lax.div(a, tok) == lax.div(b, tok)), 1.0, 0.0)
    rank = jnp.dot(
        before.astype(jnp.bfloat16), named.astype(jnp.bfloat16), preferred_element_type=jnp.float32
    )
    chosen = jnp.where(same & (named > 0.0) & (rank == rank_of), 1.0, 0.0)
    mix = chosen * weight
    high = mix.astype(jnp.bfloat16)
    low = (mix - high.astype(jnp.float32)).astype(jnp.bfloat16)
    comb_ref[0:rows, :] = high
    comb_ref[rows : 2 * rows, :] = low
    own = own_ref[...].astype(jnp.float32)
    other = other_ref[...].astype(jnp.float32)
    total = jnp.sum(own * own, axis=-1, keepdims=True) + jnp.sum(other * other, axis=-1, keepdims=True)
    scale = lax.rsqrt(total / (2 * half) + 1e-06)
    gain = gain_ref[:, pl.ds(pl.multiple_of(core * half, half), half)]
    normed = (own * scale * gain).astype(jnp.bfloat16)
    picker = chosen.T.astype(jnp.bfloat16)
    step = 256
    for at in range(0, half, step):
        send_ref[:, at : at + step] = jnp.dot(
            picker, normed[:, at : at + step], preferred_element_type=jnp.float32
        ).astype(jnp.bfloat16)


def dispatch(core, own, other, gain, meta, slots, cap, micro):
    rows, half = own.shape
    return pl.pallas_call(
        functools.partial(dispatch_body, cap, micro),
        out_shape=(
            jax.ShapeDtypeStruct((slots, half), jnp.bfloat16),
            jax.ShapeDtypeStruct((2 * rows, slots), jnp.bfloat16),
        ),
        in_specs=[pl.BlockSpec(memory_space=SMEM)] + [pl.BlockSpec(memory_space=VMEM)] * 4,
        out_specs=(pl.BlockSpec(memory_space=VMEM),) * 2,
        compiler_params=params(),
        cost_estimate=cost(2 * slots * rows * half, 2 * slots * half),
        name="dispatch",
    )(core, own, other, gain, meta)


def first_body(x_ref, wg_ref, wu_ref, g_ref, u_ref):
    g_ref[...] = jnp.dot(x_ref[...], wg_ref[...], preferred_element_type=jnp.float32)
    u_ref[...] = jnp.dot(x_ref[...], wu_ref[...], preferred_element_type=jnp.float32)


def first_half(x, wg, wu, part, tile=256):
    rows, half = x.shape
    wide = wg.shape[1]
    return pl.pallas_call(
        first_body,
        grid=(wide // tile,),
        in_specs=[
            pl.BlockSpec((rows, half), lambda n: (0, 0)),
            pl.BlockSpec((half, tile), lambda n: (part, n)),
            pl.BlockSpec((half, tile), lambda n: (part, n)),
        ],
        out_specs=[pl.BlockSpec((rows, tile), lambda n: (0, n))] * 2,
        out_shape=[jax.ShapeDtypeStruct((rows, wide), jnp.float32)] * 2,
        compiler_params=params(),
        cost_estimate=cost(4 * rows * half * wide, 4 * half * wide + 2 * rows * half),
        name="first_half",
    )(x, wg, wu)


def second_body(x_ref, wg_ref, wu_ref, g_ref, u_ref, h_ref):
    g = g_ref[...] + jnp.dot(x_ref[...], wg_ref[...], preferred_element_type=jnp.float32)
    u = u_ref[...] + jnp.dot(x_ref[...], wu_ref[...], preferred_element_type=jnp.float32)
    h_ref[...] = (jax.nn.silu(g) * u).astype(jnp.bfloat16)


def second_half(x, wg, wu, g, u, part, tile=256):
    rows, half = x.shape
    wide = wg.shape[1]
    return pl.pallas_call(
        second_body,
        grid=(wide // tile,),
        in_specs=[
            pl.BlockSpec((rows, half), lambda n: (0, 0)),
            pl.BlockSpec((half, tile), lambda n: (part, n)),
            pl.BlockSpec((half, tile), lambda n: (part, n)),
            pl.BlockSpec((rows, tile), lambda n: (0, n)),
            pl.BlockSpec((rows, tile), lambda n: (0, n)),
        ],
        out_specs=pl.BlockSpec((rows, tile), lambda n: (0, n)),
        out_shape=jax.ShapeDtypeStruct((rows, wide), jnp.bfloat16),
        compiler_params=params(),
        cost_estimate=cost(4 * rows * half * wide, 4 * half * wide + 2 * rows * half),
        name="second_half",
    )(x, wg, wu, g, u)


def down_body(h_ref, wd_ref, y_ref):
    y_ref[...] = jnp.dot(h_ref[...], wd_ref[...], preferred_element_type=jnp.float32).astype(
        jnp.bfloat16
    )


def down(h, wd, part, half, tile=512):
    rows, wide = h.shape
    return pl.pallas_call(
        down_body,
        grid=(half // tile,),
        in_specs=[
            pl.BlockSpec((rows, wide), lambda n: (0, 0)),
            pl.BlockSpec((wide, tile), lambda n: (0, part * (half // tile) + n)),
        ],
        out_specs=pl.BlockSpec((rows, tile), lambda n: (0, n)),
        out_shape=jax.ShapeDtypeStruct((rows, half), jnp.bfloat16),
        compiler_params=params(),
        cost_estimate=cost(2 * rows * half * wide, 2 * half * wide + 2 * rows * half),
        name="down",
    )(h, wd)


def combine_body(y_ref, comb_ref, own_ref, out_ref):
    rows = own_ref.shape[0]
    both = jnp.dot(comb_ref[...], y_ref[...], preferred_element_type=jnp.float32)
    mixed = own_ref[...].astype(jnp.float32) + (both[0:rows] + both[rows : 2 * rows])
    out_ref[...] = mixed.astype(jnp.bfloat16)


def combine(y, comb, own):
    rows, half = own.shape
    return pl.pallas_call(
        combine_body,
        out_shape=jax.ShapeDtypeStruct((rows, half), jnp.bfloat16),
        in_specs=[pl.BlockSpec(memory_space=VMEM)] * 3,
        out_specs=pl.BlockSpec(memory_space=VMEM),
        compiler_params=params(),
        cost_estimate=cost(4 * rows * half * y.shape[0], 2 * y.shape[0] * half),
        name="combine",
    )(y, comb, own)


def shards(tokens, expert_ids, gate_weights, norm_gain, w_gate, w_up, w_down):
    micro, tok_dev, width = tokens.shape
    top = expert_ids.shape[-1]
    groups = lax.axis_size("expert")
    segments = lax.axis_size("segment")
    rows = micro * tok_dev
    half = width // segments
    cap = 2 * tok_dev * top // groups
    slots = groups * micro * cap
    core = lax.axis_index("segment")
    core_arr = core.reshape(1).astype(jnp.int32)
    wg, wu, wd = w_gate[0, 0], w_up[0, 0], w_down[0, 0]

    meta = jnp.concatenate(
        [expert_ids.reshape(rows, top).astype(jnp.float32), gate_weights.reshape(rows, top)], axis=1
    )
    meta_other = lax.ppermute(meta, "segment", SWAP)
    gain_other = lax.ppermute(norm_gain, "segment", SWAP)
    current = tokens.reshape(rows, width)
    own = lax.dynamic_slice_in_dim(current, core * half, half, 1)
    other = lax.dynamic_slice_in_dim(current, (1 - core) * half, half, 1)
    outs = []
    for s in range(segments):
        mine = core == s
        meta_s = jnp.where(mine, meta, meta_other)
        gain_s = jnp.where(mine, norm_gain, gain_other)
        send, comb = dispatch(core_arr, own, other, gain_s, meta_s, slots, cap, micro)
        got = lax.all_to_all(
            send.reshape(groups, micro * cap, half), "expert", split_axis=0, concat_axis=0, tiled=True
        ).reshape(slots, half)
        got_other = lax.ppermute(got, "segment", [(1 - s, s)])
        g, u = first_half(got, wg, wu, s)
        hidden = second_half(got_other, wg, wu, g, u, 1 - s)
        y_other = down(hidden, wd, 1 - s, half)
        y_passed = lax.ppermute(y_other, "segment", [(s, 1 - s)])
        y_own = down(hidden, wd, s, half)
        y = jnp.where(mine, y_own, y_passed)
        back = lax.all_to_all(
            y.reshape(groups, micro * cap, half), "expert", split_axis=0, concat_axis=0, tiled=True
        ).reshape(slots, half)
        own = combine(back, comb, own)
        other = lax.ppermute(own, "segment", SWAP if s < segments - 1 else [(1 - s, s)])
        outs.append(jnp.concatenate([own, other] if s == 0 else [other, own], axis=1))
    result = jnp.where(core == 0, outs[0], outs[1])
    return result.reshape(1, micro, tok_dev, width)


def solution(mesh):
    in_specs = (
        P(None, "expert", None),
        P("segment", None, "expert", None),
        P("segment", None, "expert", None),
        P("segment", None),
        P("segment", "expert", None, None),
        P("segment", "expert", None, None),
        P("segment", "expert", None, None),
    )
    out_specs = P("segment", None, "expert", None)
    return jax.shard_map(shards, mesh=mesh, in_specs=in_specs, out_specs=out_specs, check_vma=False)
```

```python
import functools

import jax
import jax.numpy as jnp
from jax import lax
from jax.experimental import pallas as pl
from jax.experimental.pallas import tpu as pltpu
from jax.sharding import PartitionSpec as P

VMEM = pltpu.MemorySpace.VMEM
SMEM = pltpu.MemorySpace.SMEM
SWAP = [(0, 1), (1, 0)]
bf16, f32 = jnp.bfloat16, jnp.float32


def params(mib):
    return pltpu.CompilerParams(vmem_limit_bytes=mib << 20)


def cost(flops, moved):
    return pl.CostEstimate(flops=flops, bytes_accessed=moved, transcendentals=0)


def dispatch_body(cap, first, core_ref, x_ref, gain0_ref, gain1_ref, meta0_ref, meta1_ref, send_ref, comb_ref):
    slots, half = send_ref.shape
    rows = comb_ref.shape[0] // 2
    tok = rows // 2
    core = core_ref[0]
    local = core_ref[1] == 1
    if first:
        x = x_ref[core]
        x = jnp.concatenate([x[:, 0:half], x[:, half : 2 * half]], axis=0).astype(f32)
    else:
        x = x_ref[...].astype(f32)
    meta = jnp.where(local, meta0_ref[...], meta1_ref[...])
    gain = jnp.where(local, gain0_ref[...], gain1_ref[...])
    top = meta.shape[1] // 2
    meta = jnp.concatenate([meta, meta], axis=0)
    lane = lax.broadcasted_iota(jnp.int32, (rows, slots), 1)
    row = lax.broadcasted_iota(jnp.int32, (rows, slots), 0)
    expert = lax.div(lane, 2 * cap).astype(f32)
    rank_of = lax.rem(lane, cap).astype(f32)
    same = lax.rem(lax.div(lane, cap), 2) == lax.div(row, tok)
    named = jnp.zeros((rows, slots), f32)
    weight = jnp.zeros((rows, slots), f32)
    for k in range(top):
        hit = meta[:, k : k + 1] == expert
        named += jnp.where(hit, 1.0, 0.0)
        weight += jnp.where(hit, meta[:, top + k : top + k + 1], 0.0)
    a = lax.broadcasted_iota(jnp.int32, (rows, rows), 0)
    b = lax.broadcasted_iota(jnp.int32, (rows, rows), 1)
    before = jnp.where((b < a) & (lax.div(a, tok) == lax.div(b, tok)), 1.0, 0.0)
    rank = jnp.dot(before.astype(bf16), named.astype(bf16), preferred_element_type=f32)
    chosen = jnp.where(same & (named > 0.0) & (rank == rank_of), 1.0, 0.0)
    mix = chosen * weight
    high = mix.astype(bf16)
    low = (mix - high.astype(f32)).astype(bf16)
    comb_ref[0:rows, :] = high
    comb_ref[rows : 2 * rows, :] = low
    squares = jnp.sum(x * x, axis=-1, keepdims=True)
    total = squares[0:tok] + squares[tok:rows]
    scale = lax.rsqrt(total / (2 * half) + 1e-06)
    n0 = x[0:tok] * scale * gain[:, 0:half]
    n1 = x[tok:rows] * scale * gain[:, half : 2 * half]
    normed = jnp.concatenate([n0, n1], axis=0).astype(bf16)
    picker = chosen.T.astype(bf16)
    step = 256
    for at in range(0, half, step):
        send_ref[:, at : at + step] = jnp.dot(
            picker, normed[:, at : at + step], preferred_element_type=f32
        ).astype(bf16)


def dispatch(core, x, gains, metas, slots, half, cap, first):
    rows = 2 * metas[0].shape[0]
    return pl.pallas_call(
        functools.partial(dispatch_body, cap, first),
        out_shape=(
            jax.ShapeDtypeStruct((slots, half), bf16),
            jax.ShapeDtypeStruct((2 * rows, slots), bf16),
        ),
        in_specs=[pl.BlockSpec(memory_space=SMEM)] + [pl.BlockSpec(memory_space=VMEM)] * 5,
        out_specs=(pl.BlockSpec(memory_space=VMEM),) * 2,
        compiler_params=params(16),
        cost_estimate=cost(2 * slots * rows * half, 2 * slots * half),
        name="dispatch",
    )(core, x, *gains, *metas)


def placing(size, cap, back):
    wide = lax.broadcasted_iota(jnp.int32, (size, size), 1 if back else 0)
    tall = lax.broadcasted_iota(jnp.int32, (size, size), 0 if back else 1)
    part = lax.div(wide, size // 2)
    at = lax.rem(wide, size // 2)
    home = lax.div(at, cap) * (2 * cap) + part * cap + lax.rem(at, cap)
    return jnp.where(home == tall, 1.0, 0.0).astype(bf16)


def experts_body(cap, tiles, core_ref, x_ref, g0, g1, u0, u1, d0, d1, o_ref, xs, hs, wg, wu, wd, sem_g, sem_u, sem_d):
    slots, half = x_ref.shape
    wide = hs.shape[1]
    up_tile = wide // tiles
    down_tile = half // tiles_down(half)
    group = 256
    local = core_ref[1] == 1

    def copies(g, u, d):
        jobs = []
        for t in range(tiles):
            cols = pl.ds(t * up_tile, up_tile)
            jobs.append(pltpu.make_async_copy(g.at[:, cols], wg.at[:, cols], sem_g.at[t]))
            jobs.append(pltpu.make_async_copy(u.at[:, cols], wu.at[:, cols], sem_u.at[t]))
        for t in range(half // down_tile):
            for h in range(2):
                cols = pl.ds(h * half + t * down_tile, down_tile)
                jobs.append(pltpu.make_async_copy(d.at[:, cols], wd.at[:, cols], sem_d.at[2 * t + h]))
        return jobs

    @pl.when(local)
    def _():
        for job in copies(g0, u0, d0):
            job.start()

    @pl.when(jnp.logical_not(local))
    def _():
        for job in copies(g1, u1, d1):
            job.start()

    jobs = copies(g0, u0, d0)
    place = placing(group, cap, False)
    for at in range(0, slots, group):
        for col in range(0, half, 512):
            rows = jnp.dot(
                place, x_ref[at : at + group, col : col + 512], preferred_element_type=f32
            ).astype(bf16)
            xs[at // 2 : at // 2 + group // 2, col : col + 512] = rows[0 : group // 2]
            xs[at // 2 : at // 2 + group // 2, half + col : half + col + 512] = rows[group // 2 :]
    for t in range(tiles):
        jobs[2 * t].wait()
        jobs[2 * t + 1].wait()
        cols = pl.ds(t * up_tile, up_tile)
        gate = jnp.dot(xs[...], wg[:, cols], preferred_element_type=f32)
        up = jnp.dot(xs[...], wu[:, cols], preferred_element_type=f32)
        hs[:, cols] = (jax.nn.silu(gate) * up).astype(bf16)
    back = placing(group, cap, True)
    for t in range(half // down_tile):
        parts = []
        for h in range(2):
            jobs[2 * tiles + 2 * t + h].wait()
            parts.append(
                jnp.dot(
                    hs[...],
                    wd[:, pl.ds(h * half + t * down_tile, down_tile)],
                    preferred_element_type=f32,
                ).astype(bf16)
            )
        for at in range(0, slots, group):
            pair = jnp.concatenate([p[at // 2 : at // 2 + group // 2] for p in parts], axis=0)
            o_ref[at : at + group, pl.ds(t * down_tile, down_tile)] = jnp.dot(
                back, pair, preferred_element_type=f32
            ).astype(bf16)


def tiles_down(half):
    return half // 512


def experts(core, x, local, other, cap):
    slots, half = x.shape
    wide = local[0].shape[1]
    tiles = 3
    rows = slots // 2
    flops = 6 * rows * 2 * half * wide
    weights = [w for pair in zip(local, other) for w in pair]
    return pl.pallas_call(
        functools.partial(experts_body, cap, tiles),
        out_shape=jax.ShapeDtypeStruct((slots, half), bf16),
        in_specs=[pl.BlockSpec(memory_space=SMEM), pl.BlockSpec(memory_space=VMEM)]
        + [pl.BlockSpec(memory_space=pl.ANY)] * 6,
        out_specs=pl.BlockSpec(memory_space=VMEM),
        scratch_shapes=[
            pltpu.VMEM((rows, 2 * half), bf16),
            pltpu.VMEM((rows, wide), bf16),
            pltpu.VMEM((2 * half, wide), bf16),
            pltpu.VMEM((2 * half, wide), bf16),
            pltpu.VMEM((wide, 2 * half), bf16),
            pltpu.SemaphoreType.DMA((tiles,)),
            pltpu.SemaphoreType.DMA((tiles,)),
            pltpu.SemaphoreType.DMA((2 * tiles_down(half),)),
        ],
        compiler_params=params(40),
        cost_estimate=cost(flops, 6 * half * wide * 2),
        name="experts",
    )(core, x, *weights)


def combine_body(first, core_ref, y_ref, comb_ref, x_ref, out_ref):
    rows, half = out_ref.shape
    if first:
        x = x_ref[core_ref[0]]
        x = jnp.concatenate([x[:, 0:half], x[:, half : 2 * half]], axis=0).astype(f32)
    else:
        x = x_ref[...].astype(f32)
    both = jnp.dot(comb_ref[...], y_ref[...], preferred_element_type=f32)
    out_ref[...] = (x + (both[0:rows] + both[rows : 2 * rows])).astype(bf16)


def combine(core, y, comb, x, first):
    slots, half = y.shape
    rows = comb.shape[0] // 2
    return pl.pallas_call(
        functools.partial(combine_body, first),
        out_shape=jax.ShapeDtypeStruct((rows, half), bf16),
        in_specs=[pl.BlockSpec(memory_space=SMEM)] + [pl.BlockSpec(memory_space=VMEM)] * 3,
        out_specs=pl.BlockSpec(memory_space=VMEM),
        compiler_params=params(16),
        cost_estimate=cost(4 * rows * half * slots, 2 * slots * half),
        name="combine",
    )(core, y, comb, x)


def shards(tokens, expert_ids, gate_weights, norm_gain, w_gate, w_up, w_down):
    micro, tok_dev, width = tokens.shape
    top = expert_ids.shape[-1]
    groups = lax.axis_size("expert")
    segments = lax.axis_size("segment")
    half = width // 2
    cap = 2 * tok_dev * top // groups
    slots = groups * 2 * cap
    core = lax.axis_index("segment")
    swap = lambda value: lax.ppermute(value, "segment", SWAP)

    both = jnp.concatenate([expert_ids[0].astype(f32), gate_weights[0]], axis=-1)
    meta_other = swap(lax.dynamic_index_in_dim(both, 1 - core, 0, keepdims=False))
    meta = lax.dynamic_index_in_dim(both, core, 0, keepdims=False)
    gain_other = swap(norm_gain)
    local = (w_gate[0, 0], w_up[0, 0], w_down[0, 0])
    other = tuple(swap(w) for w in local)
    x = tokens
    outs = []
    for s in range(segments):
        first = s == 0
        info = jnp.stack([core, (core == s).astype(core.dtype)]).astype(jnp.int32)
        send, comb = dispatch(
            info, x, (norm_gain, gain_other), (meta, meta_other), slots, half, cap, first
        )
        got = lax.all_to_all(
            send.reshape(groups, 2 * cap, half), "expert", split_axis=0, concat_axis=0, tiled=True
        ).reshape(slots, half)
        y = experts(info, got, local, other, cap)
        back = lax.all_to_all(
            y.reshape(groups, 2 * cap, half), "expert", split_axis=0, concat_axis=0, tiled=True
        ).reshape(slots, half)
        x = combine(info, back, comb, x, first)
        outs.append(x)
    kept = jnp.where(core == 0, outs[0], outs[1])
    passed = swap(jnp.where(core == 0, outs[1], outs[0]))
    pair = [jnp.where(core == 0, kept, passed), jnp.where(core == 0, passed, kept)]
    result = jnp.stack(pair).reshape(micro, 2, tok_dev, half)
    return result.transpose(0, 2, 1, 3).reshape(1, micro, tok_dev, width)


def solution(mesh):
    in_specs = (
        P(None, "expert", None),
        P("segment", None, "expert", None),
        P("segment", None, "expert", None),
        P("segment", None),
        P("segment", "expert", None, None),
        P("segment", "expert", None, None),
        P("segment", "expert", None, None),
    )
    out_specs = P("segment", None, "expert", None)
    return jax.shard_map(shards, mesh=mesh, in_specs=in_specs, out_specs=out_specs, check_vma=False)
```

```python
import functools

import jax
import jax.numpy as jnp
from jax import lax
from jax.experimental import pallas as pl
from jax.experimental.pallas import tpu as pltpu
from jax.sharding import PartitionSpec as P

VMEM = pltpu.MemorySpace.VMEM
SMEM = pltpu.MemorySpace.SMEM
SWAP = [(0, 1), (1, 0)]
bf16, f32 = jnp.bfloat16, jnp.float32


def params(mib):
    return pltpu.CompilerParams(vmem_limit_bytes=mib << 20)


def cost(flops, moved):
    return pl.CostEstimate(flops=flops, bytes_accessed=moved, transcendentals=0)


def dispatch_body(
    cap, first, hold, core_ref, x_ref, gain0_ref, gain1_ref, ids0, ids1, gw0, gw1, send_ref, comb_ref, spun
):
    slots, half = send_ref.shape
    rows = comb_ref.shape[0] // 2
    tok = rows // 2
    core = core_ref[0]
    local = core_ref[1] == 1
    if first:
        x = x_ref[core]
        x = jnp.concatenate([x[:, 0:half], x[:, half : 2 * half]], axis=0).astype(f32)
        if hold:
            spun[...] = jnp.full(spun.shape, 0.5, f32)

            def turn(_, carry):
                spun[...] = spun[...] * 0.5 + 0.25
                return carry

            lax.fori_loop(0, core * hold, turn, 0)
    else:
        x = x_ref[...].astype(f32)
    ids = jnp.where(local, ids0[core], ids1[core]).astype(f32).T
    gates = jnp.where(local, gw0[core], gw1[core]).T
    gain = jnp.where(local, gain0_ref[...], gain1_ref[...])
    top = ids.shape[1]
    ids = jnp.concatenate([ids, ids], axis=0)
    gates = jnp.concatenate([gates, gates], axis=0)
    lane = lax.broadcasted_iota(jnp.int32, (rows, slots), 1)
    row = lax.broadcasted_iota(jnp.int32, (rows, slots), 0)
    expert = lax.div(lane, 2 * cap).astype(f32)
    rank_of = lax.rem(lane, cap).astype(f32)
    same = lax.rem(lax.div(lane, cap), 2) == lax.div(row, tok)
    named = jnp.zeros((rows, slots), f32)
    weight = jnp.zeros((rows, slots), f32)
    for k in range(top):
        hit = ids[:, k : k + 1] == expert
        named += jnp.where(hit, 1.0, 0.0)
        weight += jnp.where(hit, gates[:, k : k + 1], 0.0)
    a = lax.broadcasted_iota(jnp.int32, (rows, rows), 0)
    b = lax.broadcasted_iota(jnp.int32, (rows, rows), 1)
    before = jnp.where((b < a) & (lax.div(a, tok) == lax.div(b, tok)), 1.0, 0.0)
    rank = jnp.dot(before.astype(bf16), named.astype(bf16), preferred_element_type=f32)
    chosen = jnp.where(same & (named > 0.0) & (rank == rank_of), 1.0, 0.0)
    mix = chosen * weight
    high = mix.astype(bf16)
    low = (mix - high.astype(f32)).astype(bf16)
    comb_ref[0:rows, :] = high
    comb_ref[rows : 2 * rows, :] = low
    squares = jnp.sum(x * x, axis=-1, keepdims=True)
    total = squares[0:tok] + squares[tok:rows]
    scale = lax.rsqrt(total / (2 * half) + 1e-06)
    n0 = x[0:tok] * scale * gain[:, 0:half]
    n1 = x[tok:rows] * scale * gain[:, half : 2 * half]
    normed = jnp.concatenate([n0, n1], axis=0).astype(bf16)
    picker = chosen.T.astype(bf16)
    step = 256
    for at in range(0, half, step):
        send_ref[:, at : at + step] = jnp.dot(
            picker, normed[:, at : at + step], preferred_element_type=f32
        ).astype(bf16)


def dispatch(core, x, gains, metas, slots, half, cap, first, hold):
    rows = 2 * metas[0].shape[2]
    return pl.pallas_call(
        functools.partial(dispatch_body, cap, first, hold),
        out_shape=(
            jax.ShapeDtypeStruct((slots, half), bf16),
            jax.ShapeDtypeStruct((2 * rows, slots), bf16),
        ),
        in_specs=[pl.BlockSpec(memory_space=SMEM)] + [pl.BlockSpec(memory_space=VMEM)] * 7,
        out_specs=(pl.BlockSpec(memory_space=VMEM),) * 2,
        scratch_shapes=[pltpu.VMEM((8, 128), f32)],
        compiler_params=params(16),
        cost_estimate=cost(2 * slots * rows * half, 2 * slots * half),
        name="dispatch",
    )(core, x, *gains, *metas)


def placing(size, cap, back):
    wide = lax.broadcasted_iota(jnp.int32, (size, size), 1 if back else 0)
    tall = lax.broadcasted_iota(jnp.int32, (size, size), 0 if back else 1)
    part = lax.div(wide, size // 2)
    at = lax.rem(wide, size // 2)
    home = lax.div(at, cap) * (2 * cap) + part * cap + lax.rem(at, cap)
    return jnp.where(home == tall, 1.0, 0.0).astype(bf16)


def experts_body(cap, tiles, core_ref, x_ref, g0, g1, u0, u1, d0, d1, o_ref, xs, hs, wg, wu, wd, sems):
    slots, half = x_ref.shape
    wide = hs.shape[1]
    up_tile = wide // tiles
    down_tile = half // tiles_down(half)
    steps = tiles + tiles_down(half)
    group = 256
    local = core_ref[1] == 1

    def copies(step, g, u, d):
        if step < tiles:
            cols = [pl.ds(step * up_tile, up_tile)] * 2
            pairs = [(g, wg), (u, wu)]
        else:
            at = (step - tiles) * down_tile
            cols = [pl.ds(at, down_tile), pl.ds(half + at, down_tile)]
            pairs = [(d, wd)] * 2
        return [
            pltpu.make_async_copy(source.at[:, c], target.at[:, c], sems.at[2 * step + k])
            for k, (c, (source, target)) in enumerate(zip(cols, pairs))
        ]

    def start(step):
        if step < steps:

            @pl.when(local)
            def _():
                for job in copies(step, g0, u0, d0):
                    job.start()

            @pl.when(jnp.logical_not(local))
            def _():
                for job in copies(step, g1, u1, d1):
                    job.start()

    def wait(step):
        for job in copies(step, g0, u0, d0):
            job.wait()

    ahead = 3
    for step in range(ahead):
        start(step)
    place = placing(group, cap, False)
    for at in range(0, slots, group):
        for col in range(0, half, 512):
            rows = jnp.dot(
                place, x_ref[at : at + group, col : col + 512], preferred_element_type=f32
            ).astype(bf16)
            xs[at // 2 : at // 2 + group // 2, col : col + 512] = rows[0 : group // 2]
            xs[at // 2 : at // 2 + group // 2, half + col : half + col + 512] = rows[group // 2 :]
    for t in range(tiles):
        wait(t)
        start(t + ahead)
        cols = pl.ds(t * up_tile, up_tile)
        gate = jnp.dot(xs[...], wg[:, cols], preferred_element_type=f32)
        up = jnp.dot(xs[...], wu[:, cols], preferred_element_type=f32)
        hs[:, cols] = (jax.nn.silu(gate) * up).astype(bf16)
    back = placing(group, cap, True)
    for t in range(steps - tiles):
        wait(tiles + t)
        start(tiles + t + ahead)
        parts = [
            jnp.dot(
                hs[...],
                wd[:, pl.ds(h * half + t * down_tile, down_tile)],
                preferred_element_type=f32,
            ).astype(bf16)
            for h in range(2)
        ]
        for at in range(0, slots, group):
            pair = jnp.concatenate([p[at // 2 : at // 2 + group // 2] for p in parts], axis=0)
            o_ref[at : at + group, pl.ds(t * down_tile, down_tile)] = jnp.dot(
                back, pair, preferred_element_type=f32
            ).astype(bf16)


def tiles_down(half):
    return half // 512


def experts(core, x, local, other, cap):
    slots, half = x.shape
    wide = local[0].shape[1]
    tiles = 3
    rows = slots // 2
    flops = 6 * rows * 2 * half * wide
    weights = [w for pair in zip(local, other) for w in pair]
    return pl.pallas_call(
        functools.partial(experts_body, cap, tiles),
        out_shape=jax.ShapeDtypeStruct((slots, half), bf16),
        in_specs=[pl.BlockSpec(memory_space=SMEM), pl.BlockSpec(memory_space=VMEM)]
        + [pl.BlockSpec(memory_space=pl.ANY)] * 6,
        out_specs=pl.BlockSpec(memory_space=VMEM),
        scratch_shapes=[
            pltpu.VMEM((rows, 2 * half), bf16),
            pltpu.VMEM((rows, wide), bf16),
            pltpu.VMEM((2 * half, wide), bf16),
            pltpu.VMEM((2 * half, wide), bf16),
            pltpu.VMEM((wide, 2 * half), bf16),
            pltpu.SemaphoreType.DMA((2 * (tiles + tiles_down(half)),)),
        ],
        compiler_params=params(54),
        cost_estimate=cost(flops, 6 * half * wide * 2),
        name="experts",
    )(core, x, *weights)


def combine_body(first, core_ref, y_ref, comb_ref, x_ref, out_ref):
    rows, half = out_ref.shape
    if first:
        x = x_ref[core_ref[0]]
        x = jnp.concatenate([x[:, 0:half], x[:, half : 2 * half]], axis=0).astype(f32)
    else:
        x = x_ref[...].astype(f32)
    both = jnp.dot(comb_ref[...], y_ref[...], preferred_element_type=f32)
    out_ref[...] = (x + (both[0:rows] + both[rows : 2 * rows])).astype(bf16)


def combine(core, y, comb, x, first):
    slots, half = y.shape
    rows = comb.shape[0] // 2
    return pl.pallas_call(
        functools.partial(combine_body, first),
        out_shape=jax.ShapeDtypeStruct((rows, half), bf16),
        in_specs=[pl.BlockSpec(memory_space=SMEM)] + [pl.BlockSpec(memory_space=VMEM)] * 3,
        out_specs=pl.BlockSpec(memory_space=VMEM),
        compiler_params=params(16),
        cost_estimate=cost(4 * rows * half * slots, 2 * slots * half),
        name="combine",
    )(core, y, comb, x)


def assemble_body(core_ref, out0, out1, from1, from0, o_ref):
    core = core_ref[0]
    tok = o_ref.shape[1]
    half = out0.shape[1]

    @pl.when(core == 0)
    def _():
        for h in range(2):
            o_ref[0, :, h * half : (h + 1) * half] = out0[h * tok : (h + 1) * tok, :]
            o_ref[1, :, h * half : (h + 1) * half] = from1[h * tok : (h + 1) * tok, :]

    @pl.when(core == 1)
    def _():
        for h in range(2):
            o_ref[0, :, h * half : (h + 1) * half] = from0[h * tok : (h + 1) * tok, :]
            o_ref[1, :, h * half : (h + 1) * half] = out1[h * tok : (h + 1) * tok, :]


def assemble(core, out0, out1, from1, from0, shape):
    return pl.pallas_call(
        assemble_body,
        out_shape=jax.ShapeDtypeStruct(shape, bf16),
        in_specs=[pl.BlockSpec(memory_space=SMEM)] + [pl.BlockSpec(memory_space=VMEM)] * 4,
        out_specs=pl.BlockSpec(memory_space=VMEM),
        compiler_params=params(8),
        name="assemble",
    )(core, out0, out1, from1, from0)


HOLD = 2000


def shards(tokens, expert_ids, gate_weights, norm_gain, w_gate, w_up, w_down):
    micro, tok_dev, width = tokens.shape
    top = expert_ids.shape[-1]
    groups = lax.axis_size("expert")
    segments = lax.axis_size("segment")
    half = width // 2
    cap = 2 * tok_dev * top // groups
    slots = groups * 2 * cap
    core = lax.axis_index("segment")
    swap = lambda value: lax.ppermute(value, "segment", SWAP)

    ids = expert_ids[0].transpose(0, 2, 1)
    gates = gate_weights[0].transpose(0, 2, 1)
    ids_other, gates_other, gain_other = swap(ids), swap(gates), swap(norm_gain)
    local = (w_gate[0, 0], w_up[0, 0], w_down[0, 0])
    *tied, ids_other, gates_other, gain_other = lax.optimization_barrier(
        (*local, ids_other, gates_other, gain_other)
    )
    other = tuple(swap(w) for w in tied)
    x = tokens
    outs = []
    for s in range(segments):
        first = s == 0
        info = jnp.stack([core, (core == s).astype(core.dtype)]).astype(jnp.int32)
        send, comb = dispatch(
            info,
            x,
            (norm_gain, gain_other),
            (ids, ids_other, gates, gates_other),
            slots,
            half,
            cap,
            first,
            HOLD,
        )
        got = lax.all_to_all(
            send.reshape(groups, 2 * cap, half), "expert", split_axis=0, concat_axis=0, tiled=True
        ).reshape(slots, half)
        y = experts(info, got, local, other, cap)
        back = lax.all_to_all(
            y.reshape(groups, 2 * cap, half), "expert", split_axis=0, concat_axis=0, tiled=True
        ).reshape(slots, half)
        x = combine(info, back, comb, x, first)
        outs.append(x)
    from1 = lax.ppermute(outs[0], "segment", [(1, 0)])
    from0 = lax.ppermute(outs[1], "segment", [(0, 1)])
    return assemble(info, outs[0], outs[1], from1, from0, (micro, tok_dev, width))[None]


def solution(mesh):
    in_specs = (
        P(None, "expert", None),
        P("segment", None, "expert", None),
        P("segment", None, "expert", None),
        P("segment", None),
        P("segment", "expert", None, None),
        P("segment", "expert", None, None),
        P("segment", "expert", None, None),
    )
    out_specs = P("segment", None, "expert", None)
    return jax.shard_map(shards, mesh=mesh, in_specs=in_specs, out_specs=out_specs, check_vma=False)
```

```python
import functools

import jax
import jax.numpy as jnp
from jax import lax
from jax.experimental import pallas as pl
from jax.experimental.pallas import tpu as pltpu
from jax.sharding import PartitionSpec as P

VMEM = pltpu.MemorySpace.VMEM
SMEM = pltpu.MemorySpace.SMEM
HBM = pltpu.MemorySpace.HBM
SWAP = [(0, 1), (1, 0)]
SMALL_IN = [HBM, HBM, pl.ANY, HBM, pl.ANY, HBM, pl.ANY]
bf16, f32 = jnp.bfloat16, jnp.float32


def params(mib):
    return pltpu.CompilerParams(vmem_limit_bytes=mib << 20)


def cost(flops, moved):
    return pl.CostEstimate(flops=flops, bytes_accessed=moved, transcendentals=0)


def fetch_small(core_ref, section_sources, scratch, sems):
    core = core_ref[0]
    local = core_ref[1] == 1
    mine, theirs = section_sources[0::2], section_sources[1::2]

    def jobs(sources):
        picked = [sources[0], sources[1].at[core], sources[2].at[core]]
        return [
            pltpu.make_async_copy(source, target, sems.at[k])
            for k, (source, target) in enumerate(zip(picked, scratch))
        ]

    @pl.when(local)
    def _():
        for job in jobs(mine):
            job.start()

    @pl.when(jnp.logical_not(local))
    def _():
        for job in jobs(theirs):
            job.start()

    return jobs(mine)


def route(cap, ids, gates, slots):
    ids = ids.astype(f32).T
    gates = gates.T
    tok, top = ids.shape
    rows = 2 * tok
    ids = jnp.concatenate([ids, ids], axis=0)
    gates = jnp.concatenate([gates, gates], axis=0)
    lane = lax.broadcasted_iota(jnp.int32, (rows, slots), 1)
    row = lax.broadcasted_iota(jnp.int32, (rows, slots), 0)
    expert = lax.div(lane, 2 * cap).astype(f32)
    rank_of = lax.rem(lane, cap).astype(f32)
    same = lax.rem(lax.div(lane, cap), 2) == lax.div(row, tok)
    named = jnp.zeros((rows, slots), f32)
    weight = jnp.zeros((rows, slots), f32)
    for k in range(top):
        hit = ids[:, k : k + 1] == expert
        named += jnp.where(hit, 1.0, 0.0)
        weight += jnp.where(hit, gates[:, k : k + 1], 0.0)
    a = lax.broadcasted_iota(jnp.int32, (rows, rows), 0)
    b = lax.broadcasted_iota(jnp.int32, (rows, rows), 1)
    before = jnp.where((b < a) & (lax.div(a, tok) == lax.div(b, tok)), 1.0, 0.0)
    rank = jnp.dot(before.astype(bf16), named.astype(bf16), preferred_element_type=f32)
    chosen = jnp.where(same & (named > 0.0) & (rank == rank_of), 1.0, 0.0)
    return chosen, chosen * weight


def put_rows(x, gain, chosen, mix, send_ref, comb_ref):
    rows, half = x.shape
    tok = rows // 2
    high = mix.astype(bf16)
    comb_ref[0:rows, :] = high
    comb_ref[rows : 2 * rows, :] = (mix - high.astype(f32)).astype(bf16)
    squares = jnp.sum(x * x, axis=-1, keepdims=True)
    scale = lax.rsqrt((squares[0:tok] + squares[tok:rows]) / (2 * half) + 1e-06)
    n0 = x[0:tok] * scale * gain[:, 0:half]
    n1 = x[tok:rows] * scale * gain[:, half : 2 * half]
    normed = jnp.concatenate([n0, n1], axis=0).astype(bf16)
    picker = chosen.T.astype(bf16)
    step = 256
    for at in range(0, half, step):
        send_ref[:, at : at + step] = jnp.dot(
            picker, normed[:, at : at + step], preferred_element_type=f32
        ).astype(bf16)


def stacked(x):
    half = x.shape[1] // 2
    return jnp.concatenate([x[:, 0:half], x[:, half : 2 * half]], axis=0).astype(f32)


def begin_body(
    cap, hold, core_ref, tokens, n0, n1, i0, i1, w0, w1, send_ref, comb_ref, x_s, gain_s, ids_s, gw_s, spun, sems
):
    core = core_ref[0]
    jobs = [pltpu.make_async_copy(tokens.at[core], x_s, sems.at[3])]
    jobs[0].start()
    jobs += fetch_small(core_ref, (n0, n1, i0, i1, w0, w1), (gain_s, ids_s, gw_s), sems)
    spun[...] = jnp.full(spun.shape, 0.5, f32)

    def turn(_, carry):
        spun[...] = spun[...] * 0.5 + 0.25
        return carry

    lax.fori_loop(0, core * hold, turn, 0)
    for job in jobs:
        job.wait()
    chosen, mix = route(cap, ids_s[...], gw_s[...], send_ref.shape[0])
    put_rows(stacked(x_s[...]), gain_s[...], chosen, mix, send_ref, comb_ref)


def begin(core, tokens, small, slots, half, cap, hold):
    tok, width = tokens.shape[1:]
    top = small[2].shape[1]
    return pl.pallas_call(
        functools.partial(begin_body, cap, hold),
        out_shape=(
            jax.ShapeDtypeStruct((slots, half), bf16),
            jax.ShapeDtypeStruct((4 * tok, slots), bf16),
        ),
        in_specs=[pl.BlockSpec(memory_space=SMEM)]
        + [pl.BlockSpec(memory_space=m) for m in SMALL_IN],
        out_specs=(pl.BlockSpec(memory_space=VMEM),) * 2,
        scratch_shapes=[
            pltpu.VMEM((tok, width), bf16),
            pltpu.VMEM((1, width), f32),
            pltpu.VMEM((top, tok), jnp.int32),
            pltpu.VMEM((top, tok), f32),
            pltpu.VMEM((8, 128), f32),
            pltpu.SemaphoreType.DMA((4,)),
        ],
        compiler_params=params(8),
        cost_estimate=cost(LONG, 2 * slots * half),
        name="begin",
    )(core, tokens, *small)


def mixed(y_ref, comb_ref):
    both = jnp.dot(comb_ref[...], y_ref[...], preferred_element_type=f32)
    rows = both.shape[0] // 2
    return both[0:rows] + both[rows : 2 * rows]


def middle_body(
    cap, core_ref, y_ref, old_ref, tokens, n0, n1, i0, i1, w0, w1, x_ref, send_ref, comb_ref, x_s, gain_s, ids_s, gw_s, sems
):
    jobs = [pltpu.make_async_copy(tokens.at[core_ref[0]], x_s, sems.at[3])]
    jobs[0].start()
    jobs += fetch_small(core_ref, (n0, n1, i0, i1, w0, w1), (gain_s, ids_s, gw_s), sems)
    added = mixed(y_ref, old_ref)
    for job in jobs:
        job.wait()
    chosen, mix = route(cap, ids_s[...], gw_s[...], send_ref.shape[0])
    x = (stacked(x_s[...]) + added).astype(bf16)
    x_ref[...] = x
    put_rows(x.astype(f32), gain_s[...], chosen, mix, send_ref, comb_ref)


def middle(core, y, old, tokens, small, cap):
    slots, half = y.shape
    tok, width = tokens.shape[1:]
    top = small[2].shape[1]
    return pl.pallas_call(
        functools.partial(middle_body, cap),
        out_shape=(
            jax.ShapeDtypeStruct((2 * tok, half), bf16),
            jax.ShapeDtypeStruct((slots, half), bf16),
            jax.ShapeDtypeStruct((4 * tok, slots), bf16),
        ),
        in_specs=[pl.BlockSpec(memory_space=SMEM)]
        + [pl.BlockSpec(memory_space=VMEM)] * 2
        + [pl.BlockSpec(memory_space=m) for m in SMALL_IN],
        out_specs=(pl.BlockSpec(memory_space=VMEM),) * 3,
        scratch_shapes=[
            pltpu.VMEM((tok, width), bf16),
            pltpu.VMEM((1, width), f32),
            pltpu.VMEM((top, tok), jnp.int32),
            pltpu.VMEM((top, tok), f32),
            pltpu.SemaphoreType.DMA((4,)),
        ],
        compiler_params=params(8),
        cost_estimate=cost(LONG, 4 * slots * half),
        name="middle",
    )(core, y, old, tokens, *small)


def placing(size, cap, back):
    wide = lax.broadcasted_iota(jnp.int32, (size, size), 1 if back else 0)
    tall = lax.broadcasted_iota(jnp.int32, (size, size), 0 if back else 1)
    part = lax.div(wide, size // 2)
    at = lax.rem(wide, size // 2)
    home = lax.div(at, cap) * (2 * cap) + part * cap + lax.rem(at, cap)
    return jnp.where(home == tall, 1.0, 0.0).astype(bf16)


def experts_body(cap, tiles, ahead, resident, core_ref, x_ref, g0, u0, d0, g1, u1, d1, o_ref, xs, hs, ob, sems, *streams):
    slots, half = x_ref.shape
    wide = hs.shape[1]
    up_tile = wide // tiles
    down_tile = half // tiles_down(half)
    steps = tiles + tiles_down(half)
    group = 256
    local = core_ref[1] == 1

    def copies(step):
        wg, wu, wd = streams
        if step < tiles:
            cols = [pl.ds(step * up_tile, up_tile)] * 2
            pairs = [(g1, wg), (u1, wu)]
        else:
            at = (step - tiles) * down_tile
            cols = [pl.ds(at, down_tile), pl.ds(half + at, down_tile)]
            pairs = [(d1, wd)] * 2
        return [
            pltpu.make_async_copy(source.at[:, c], target.at[:, c], sems.at[2 * step + k])
            for k, (c, (source, target)) in enumerate(zip(cols, pairs))
        ]

    def start(step):
        if step < steps:
            for job in copies(step):
                job.start()

    def wait(step):
        for job in copies(step):
            job.wait()

    if not resident:

        @pl.when(jnp.logical_not(local))
        def _():
            for step in range(ahead):
                start(step)

    place = placing(group, cap, False)
    back = placing(group, cap, True)
    for at in range(0, slots, group):
        for col in range(0, half, 512):
            rows = jnp.dot(
                place, x_ref[at : at + group, col : col + 512], preferred_element_type=f32
            ).astype(bf16)
            xs[at // 2 : at // 2 + group // 2, col : col + 512] = rows[0 : group // 2]
            xs[at // 2 : at // 2 + group // 2, half + col : half + col + 512] = rows[group // 2 :]

    def run(g, u, d, fetched):
        for t in range(tiles):
            if fetched:
                wait(t)
                start(t + ahead)
            cols = pl.ds(t * up_tile, up_tile)
            gate = jnp.dot(xs[...], g[:, cols], preferred_element_type=f32)
            up = jnp.dot(xs[...], u[:, cols], preferred_element_type=f32)
            hs[:, cols] = (jax.nn.silu(gate) * up).astype(bf16)
        leaving = []
        for t in range(steps - tiles):
            if fetched:
                wait(tiles + t)
                start(tiles + t + ahead)
            cols = pl.ds(t * down_tile, down_tile)
            parts = [
                jnp.dot(
                    hs[...],
                    d[:, pl.ds(h * half + t * down_tile, down_tile)],
                    preferred_element_type=f32,
                ).astype(bf16)
                for h in range(2)
            ]
            for at in range(0, slots, group):
                pair = jnp.concatenate([p[at // 2 : at // 2 + group // 2] for p in parts], axis=0)
                ob[at : at + group, cols] = jnp.dot(
                    back, pair, preferred_element_type=f32
                ).astype(bf16)
            leaving.append(
                pltpu.make_async_copy(ob.at[:, cols], o_ref.at[:, cols], sems.at[2 * steps + t])
            )
            leaving[-1].start()
        for job in leaving:
            job.wait()

    @pl.when(local)
    def _():
        run(g0, u0, d0, False)

    @pl.when(jnp.logical_not(local))
    def _():
        run(*((g1, u1, d1) if resident else streams), not resident)


def tiles_down(half):
    return half // 512


def experts(core, x, local, other, cap, resident):
    slots, half = x.shape
    wide = local[0].shape[1]
    tiles = 3
    rows = slots // 2
    flops = 6 * rows * 2 * half * wide
    if not resident:
        other = tuple(pltpu.with_memory_space_constraint(w, HBM) for w in other)
    return pl.pallas_call(
        functools.partial(experts_body, cap, tiles, AHEAD, resident),
        out_shape=jax.ShapeDtypeStruct((slots, half), bf16),
        in_specs=[pl.BlockSpec(memory_space=SMEM)]
        + [pl.BlockSpec(memory_space=VMEM)] * 4
        + [pl.BlockSpec(memory_space=VMEM if resident else pl.ANY)] * 3,
        out_specs=pl.BlockSpec(memory_space=pl.ANY),
        scratch_shapes=[
            pltpu.VMEM((rows, 2 * half), bf16),
            pltpu.VMEM((rows, wide), bf16),
            pltpu.VMEM((slots, half), bf16),
            pltpu.SemaphoreType.DMA((2 * tiles + 3 * tiles_down(half),)),
        ]
        + ([] if resident else [pltpu.VMEM(w.shape, bf16) for w in other]),
        compiler_params=params(7 if resident else 26),
        cost_estimate=cost(flops, 6 * half * wide * 2),
        name="experts",
    )(core, x, *local, *other)


def combine_body(y_ref, comb_ref, x_ref, out_ref):
    out_ref[...] = (x_ref[...].astype(f32) + mixed(y_ref, comb_ref)).astype(bf16)


def combine(y, comb, x):
    slots, half = y.shape
    return pl.pallas_call(
        combine_body,
        out_shape=jax.ShapeDtypeStruct(x.shape, bf16),
        in_specs=[pl.BlockSpec(memory_space=VMEM)] * 3,
        out_specs=pl.BlockSpec(memory_space=VMEM),
        compiler_params=params(8),
        cost_estimate=cost(4 * x.shape[0] * half * slots, 2 * slots * half),
        name="combine",
    )(y, comb, x)


def assemble_body(core_ref, out0, out1, from1, from0, o_ref):
    core = core_ref[0]
    tok = o_ref.shape[1]
    half = out0.shape[1]

    @pl.when(core == 0)
    def _():
        for h in range(2):
            o_ref[0, :, h * half : (h + 1) * half] = out0[h * tok : (h + 1) * tok, :]
            o_ref[1, :, h * half : (h + 1) * half] = from1[h * tok : (h + 1) * tok, :]

    @pl.when(core == 1)
    def _():
        for h in range(2):
            o_ref[0, :, h * half : (h + 1) * half] = from0[h * tok : (h + 1) * tok, :]
            o_ref[1, :, h * half : (h + 1) * half] = out1[h * tok : (h + 1) * tok, :]


def assemble(core, out0, out1, from1, from0, shape):
    return pl.pallas_call(
        assemble_body,
        out_shape=jax.ShapeDtypeStruct(shape, bf16),
        in_specs=[pl.BlockSpec(memory_space=SMEM)] + [pl.BlockSpec(memory_space=VMEM)] * 4,
        out_specs=pl.BlockSpec(memory_space=VMEM),
        compiler_params=params(8),
        name="assemble",
    )(core, out0, out1, from1, from0)


HOLD = 2000
AHEAD = 2
RESIDENT = False
LONG = 1 << 35


def shards(tokens, expert_ids, gate_weights, norm_gain, w_gate, w_up, w_down):
    micro, tok_dev, width = tokens.shape
    top = expert_ids.shape[-1]
    groups = lax.axis_size("expert")
    half = width // 2
    cap = 2 * tok_dev * top // groups
    slots = groups * 2 * cap
    core = lax.axis_index("segment")
    swap = lambda value: lax.ppermute(value, "segment", SWAP)

    def travel(rows):
        boxes = rows.reshape(groups, 2 * cap, half)
        return lax.all_to_all(
            boxes, "expert", split_axis=0, concat_axis=0, tiled=True
        ).reshape(slots, half)

    ids = expert_ids[0].transpose(0, 2, 1)
    gates = gate_weights[0].transpose(0, 2, 1)
    ids_other, gates_other, gain_other = swap(ids), swap(gates), swap(norm_gain)
    local = (w_gate[0, 0], w_up[0, 0], w_down[0, 0])
    *tied, ids_other, gates_other, gain_other = lax.optimization_barrier(
        (*local, ids_other, gates_other, gain_other)
    )
    other = tuple(swap(w) for w in tied)
    pin = lambda value: pltpu.with_memory_space_constraint(value, HBM)
    small = (pin(norm_gain), gain_other, pin(ids), ids_other, pin(gates), gates_other)
    tokens = pin(tokens)
    info = [jnp.stack([core, (core == s).astype(core.dtype)]).astype(jnp.int32) for s in range(2)]
    info = lax.optimization_barrier(info)
    send, comb0 = begin(info[0], tokens, small, slots, half, cap, HOLD)
    y = experts(info[0], travel(send), local, other, cap, False)
    out0, send, comb1 = middle(info[1], travel(y), comb0, tokens, small, cap)
    y = experts(info[1], travel(send), local, other, cap, RESIDENT)
    out1 = combine(travel(y), comb1, out0)
    out0, out1 = lax.optimization_barrier((out0, out1))
    from1 = lax.ppermute(out0, "segment", [(1, 0)])
    from0 = lax.ppermute(out1, "segment", [(0, 1)])
    return assemble(info[0], out0, out1, from1, from0, (micro, tok_dev, width))[None]


def solution(mesh):
    in_specs = (
        P(None, "expert", None),
        P("segment", None, "expert", None),
        P("segment", None, "expert", None),
        P("segment", None),
        P("segment", "expert", None, None),
        P("segment", "expert", None, None),
        P("segment", "expert", None, None),
    )
    out_specs = P("segment", None, "expert", None)
    return jax.shard_map(shards, mesh=mesh, in_specs=in_specs, out_specs=out_specs, check_vma=False)
```

```python
import functools

import jax
import jax.numpy as jnp
from jax import lax
from jax.experimental import pallas as pl
from jax.experimental.pallas import tpu as pltpu
from jax.sharding import PartitionSpec as P

VMEM = pltpu.MemorySpace.VMEM
SMEM = pltpu.MemorySpace.SMEM
HBM = pltpu.MemorySpace.HBM
SWAP = [(0, 1), (1, 0)]
SMALL_IN = [HBM, HBM, pl.ANY, HBM, pl.ANY, HBM, pl.ANY]
bf16, f32 = jnp.bfloat16, jnp.float32


def params(mib):
    return pltpu.CompilerParams(vmem_limit_bytes=mib << 20)


def cost(flops, moved):
    return pl.CostEstimate(flops=flops, bytes_accessed=moved, transcendentals=0)


def fetch_small(core_ref, section_sources, scratch, sems):
    core = core_ref[0]
    local = core_ref[1] == 1
    mine, theirs = section_sources[0::2], section_sources[1::2]

    def jobs(sources):
        picked = [sources[0], sources[1].at[core], sources[2].at[core]]
        return [
            pltpu.make_async_copy(source, target, sems.at[k])
            for k, (source, target) in enumerate(zip(picked, scratch))
        ]

    @pl.when(local)
    def _():
        for job in jobs(mine):
            job.start()

    @pl.when(jnp.logical_not(local))
    def _():
        for job in jobs(theirs):
            job.start()

    return jobs(mine)


def route(cap, ids, gates, slots):
    ids = ids.astype(f32).T
    gates = gates.T
    tok, top = ids.shape
    rows = 2 * tok
    ids = jnp.concatenate([ids, ids], axis=0)
    gates = jnp.concatenate([gates, gates], axis=0)
    lane = lax.broadcasted_iota(jnp.int32, (rows, slots), 1)
    row = lax.broadcasted_iota(jnp.int32, (rows, slots), 0)
    expert = lax.div(lane, 2 * cap).astype(f32)
    rank_of = lax.rem(lane, cap).astype(f32)
    same = lax.rem(lax.div(lane, cap), 2) == lax.div(row, tok)
    named = jnp.zeros((rows, slots), f32)
    weight = jnp.zeros((rows, slots), f32)
    for k in range(top):
        hit = ids[:, k : k + 1] == expert
        named += jnp.where(hit, 1.0, 0.0)
        weight += jnp.where(hit, gates[:, k : k + 1], 0.0)
    a = lax.broadcasted_iota(jnp.int32, (rows, rows), 0)
    b = lax.broadcasted_iota(jnp.int32, (rows, rows), 1)
    before = jnp.where((b < a) & (lax.div(a, tok) == lax.div(b, tok)), 1.0, 0.0)
    rank = jnp.dot(before.astype(bf16), named.astype(bf16), preferred_element_type=f32)
    chosen = jnp.where(same & (named > 0.0) & (rank == rank_of), 1.0, 0.0)
    return chosen, chosen * weight


def put_rows(x, gain, chosen, mix, send_ref, comb_ref):
    rows, half = x.shape
    tok = rows // 2
    high = mix.astype(bf16)
    comb_ref[0:rows, :] = high
    comb_ref[rows : 2 * rows, :] = (mix - high.astype(f32)).astype(bf16)
    squares = jnp.sum(x * x, axis=-1, keepdims=True)
    scale = lax.rsqrt((squares[0:tok] + squares[tok:rows]) / (2 * half) + 1e-06)
    n0 = x[0:tok] * scale * gain[:, 0:half]
    n1 = x[tok:rows] * scale * gain[:, half : 2 * half]
    normed = jnp.concatenate([n0, n1], axis=0).astype(bf16)
    picker = chosen.T.astype(bf16)
    step = 256
    for at in range(0, half, step):
        send_ref[:, at : at + step] = jnp.dot(
            picker, normed[:, at : at + step], preferred_element_type=f32
        ).astype(bf16)


def stacked(x):
    half = x.shape[1] // 2
    return jnp.concatenate([x[:, 0:half], x[:, half : 2 * half]], axis=0).astype(f32)


def begin_body(
    cap, hold, core_ref, tokens, n0, n1, i0, i1, w0, w1, send_ref, comb_ref, x_s, gain_s, ids_s, gw_s, spun, sems
):
    core = core_ref[0]
    jobs = [pltpu.make_async_copy(tokens.at[core], x_s, sems.at[3])]
    jobs[0].start()
    jobs += fetch_small(core_ref, (n0, n1, i0, i1, w0, w1), (gain_s, ids_s, gw_s), sems)
    spun[...] = jnp.full(spun.shape, 0.5, f32)

    def turn(_, carry):
        spun[...] = spun[...] * 0.5 + 0.25
        return carry

    lax.fori_loop(0, core * hold, turn, 0)
    for job in jobs:
        job.wait()
    chosen, mix = route(cap, ids_s[...], gw_s[...], send_ref.shape[0])
    put_rows(stacked(x_s[...]), gain_s[...], chosen, mix, send_ref, comb_ref)


def begin(core, tokens, small, slots, half, cap, hold):
    tok, width = tokens.shape[1:]
    top = small[2].shape[1]
    return pl.pallas_call(
        functools.partial(begin_body, cap, hold),
        out_shape=(
            jax.ShapeDtypeStruct((slots, half), bf16),
            jax.ShapeDtypeStruct((4 * tok, slots), bf16),
        ),
        in_specs=[pl.BlockSpec(memory_space=SMEM)]
        + [pl.BlockSpec(memory_space=m) for m in SMALL_IN],
        out_specs=(pl.BlockSpec(memory_space=VMEM),) * 2,
        scratch_shapes=[
            pltpu.VMEM((tok, width), bf16),
            pltpu.VMEM((1, width), f32),
            pltpu.VMEM((top, tok), jnp.int32),
            pltpu.VMEM((top, tok), f32),
            pltpu.VMEM((8, 128), f32),
            pltpu.SemaphoreType.DMA((4,)),
        ],
        compiler_params=params(8),
        cost_estimate=cost(LONG, 2 * slots * half),
        name="begin",
    )(core, tokens, *small)


def mixed(y_ref, comb_ref):
    both = jnp.dot(comb_ref[...], y_ref[...], preferred_element_type=f32)
    rows = both.shape[0] // 2
    return both[0:rows] + both[rows : 2 * rows]


def middle_body(
    cap, core_ref, y_ref, old_ref, tokens, n0, n1, i0, i1, w0, w1, x_ref, send_ref, comb_ref, x_s, gain_s, ids_s, gw_s, sems
):
    jobs = [pltpu.make_async_copy(tokens.at[core_ref[0]], x_s, sems.at[3])]
    jobs[0].start()
    jobs += fetch_small(core_ref, (n0, n1, i0, i1, w0, w1), (gain_s, ids_s, gw_s), sems)
    added = mixed(y_ref, old_ref)
    for job in jobs:
        job.wait()
    chosen, mix = route(cap, ids_s[...], gw_s[...], send_ref.shape[0])
    x = (stacked(x_s[...]) + added).astype(bf16)
    x_ref[...] = x
    put_rows(x.astype(f32), gain_s[...], chosen, mix, send_ref, comb_ref)


def middle(core, y, old, tokens, small, cap):
    slots, half = y.shape
    tok, width = tokens.shape[1:]
    top = small[2].shape[1]
    return pl.pallas_call(
        functools.partial(middle_body, cap),
        out_shape=(
            jax.ShapeDtypeStruct((2 * tok, half), bf16),
            jax.ShapeDtypeStruct((slots, half), bf16),
            jax.ShapeDtypeStruct((4 * tok, slots), bf16),
        ),
        in_specs=[pl.BlockSpec(memory_space=SMEM)]
        + [pl.BlockSpec(memory_space=VMEM)] * 2
        + [pl.BlockSpec(memory_space=m) for m in SMALL_IN],
        out_specs=(pl.BlockSpec(memory_space=VMEM),) * 3,
        scratch_shapes=[
            pltpu.VMEM((tok, width), bf16),
            pltpu.VMEM((1, width), f32),
            pltpu.VMEM((top, tok), jnp.int32),
            pltpu.VMEM((top, tok), f32),
            pltpu.SemaphoreType.DMA((4,)),
        ],
        compiler_params=params(8),
        cost_estimate=cost(LONG, 4 * slots * half),
        name="middle",
    )(core, y, old, tokens, *small)


def placing(size, cap, back):
    wide = lax.broadcasted_iota(jnp.int32, (size, size), 1 if back else 0)
    tall = lax.broadcasted_iota(jnp.int32, (size, size), 0 if back else 1)
    part = lax.div(wide, size // 2)
    at = lax.rem(wide, size // 2)
    home = lax.div(at, cap) * (2 * cap) + part * cap + lax.rem(at, cap)
    return jnp.where(home == tall, 1.0, 0.0).astype(bf16)


def experts_body(cap, tiles, ahead, resident, core_ref, x_ref, g0, u0, d0, g1, u1, d1, o_ref, xs, hs, sems, *streams):
    slots, half = x_ref.shape
    wide = hs.shape[1]
    up_tile = wide // tiles
    down_tile = half // tiles_down(half)
    steps = tiles + tiles_down(half)
    group = 256
    local = core_ref[1] == 1

    def copies(step):
        wg, wu, wd = streams
        if step < tiles:
            cols = [pl.ds(step * up_tile, up_tile)] * 2
            pairs = [(g1, wg), (u1, wu)]
        else:
            at = (step - tiles) * down_tile
            cols = [pl.ds(at, down_tile), pl.ds(half + at, down_tile)]
            pairs = [(d1, wd)] * 2
        return [
            pltpu.make_async_copy(source.at[:, c], target.at[:, c], sems.at[2 * step + k])
            for k, (c, (source, target)) in enumerate(zip(cols, pairs))
        ]

    def start(step):
        if step < steps:
            for job in copies(step):
                job.start()

    def wait(step):
        for job in copies(step):
            job.wait()

    if not resident:

        @pl.when(jnp.logical_not(local))
        def _():
            for step in range(ahead):
                start(step)

    place = placing(group, cap, False)
    back = placing(group, cap, True)
    for at in range(0, slots, group):
        for col in range(0, half, 512):
            rows = jnp.dot(
                place, x_ref[at : at + group, col : col + 512], preferred_element_type=f32
            ).astype(bf16)
            xs[at // 2 : at // 2 + group // 2, col : col + 512] = rows[0 : group // 2]
            xs[at // 2 : at // 2 + group // 2, half + col : half + col + 512] = rows[group // 2 :]

    def run(g, u, d, fetched):
        for t in range(tiles):
            if fetched:
                wait(t)
                start(t + ahead)
            cols = pl.ds(t * up_tile, up_tile)
            gate = jnp.dot(xs[...], g[:, cols], preferred_element_type=f32)
            up = jnp.dot(xs[...], u[:, cols], preferred_element_type=f32)
            hs[:, cols] = (jax.nn.silu(gate) * up).astype(bf16)
        for t in range(steps - tiles):
            if fetched:
                wait(tiles + t)
                start(tiles + t + ahead)
            cols = pl.ds(t * down_tile, down_tile)
            parts = [
                jnp.dot(
                    hs[...],
                    d[:, pl.ds(h * half + t * down_tile, down_tile)],
                    preferred_element_type=f32,
                ).astype(bf16)
                for h in range(2)
            ]
            for at in range(0, slots, group):
                pair = jnp.concatenate([p[at // 2 : at // 2 + group // 2] for p in parts], axis=0)
                o_ref[at : at + group, cols] = jnp.dot(
                    back, pair, preferred_element_type=f32
                ).astype(bf16)

    @pl.when(local)
    def _():
        run(g0, u0, d0, False)

    @pl.when(jnp.logical_not(local))
    def _():
        run(*((g1, u1, d1) if resident else streams), not resident)


def tiles_down(half):
    return half // 512


def experts(core, x, local, other, cap, resident):
    slots, half = x.shape
    wide = local[0].shape[1]
    tiles = 3
    rows = slots // 2
    flops = 6 * rows * 2 * half * wide
    if not resident:
        other = tuple(pltpu.with_memory_space_constraint(w, HBM) for w in other)
    return pl.pallas_call(
        functools.partial(experts_body, cap, tiles, AHEAD, resident),
        out_shape=jax.ShapeDtypeStruct((slots, half), bf16),
        in_specs=[pl.BlockSpec(memory_space=SMEM)]
        + [pl.BlockSpec(memory_space=VMEM)] * 4
        + [pl.BlockSpec(memory_space=VMEM if resident else pl.ANY)] * 3,
        out_specs=pl.BlockSpec(memory_space=VMEM),
        scratch_shapes=[
            pltpu.VMEM((rows, 2 * half), bf16),
            pltpu.VMEM((rows, wide), bf16),
            pltpu.SemaphoreType.DMA((2 * tiles + 2 * tiles_down(half),)),
        ]
        + ([] if resident else [pltpu.VMEM(w.shape, bf16) for w in other]),
        compiler_params=params(7 if resident else 26),
        cost_estimate=cost(flops, 6 * half * wide * 2),
        name="experts",
    )(core, x, *local, *other)


def combine_body(core_ref, y_ref, comb_ref, x_ref, out_ref, pass_ref):
    x = x_ref[...]
    out = (x.astype(f32) + mixed(y_ref, comb_ref)).astype(bf16)
    out_ref[...] = out
    pass_ref[...] = jnp.where(core_ref[0] == 0, out, x)


def combine(core, y, comb, x):
    slots, half = y.shape
    return pl.pallas_call(
        combine_body,
        out_shape=(jax.ShapeDtypeStruct(x.shape, bf16),) * 2,
        in_specs=[pl.BlockSpec(memory_space=SMEM)] + [pl.BlockSpec(memory_space=VMEM)] * 3,
        out_specs=(pl.BlockSpec(memory_space=VMEM),) * 2,
        compiler_params=params(6),
        cost_estimate=cost(4 * x.shape[0] * half * slots, 2 * slots * half),
        name="combine",
    )(core, y, comb, x)


def assemble_body(core_ref, out0, out1, got, o_ref):
    core = core_ref[0]
    tok = o_ref.shape[1]
    half = out0.shape[1]
    for h in range(2):
        rows, cols = slice(h * tok, (h + 1) * tok), slice(h * half, (h + 1) * half)
        mine = jnp.where(core == 0, out0[rows, :], out1[rows, :])
        o_ref[core, :, cols] = mine
        o_ref[1 - core, :, cols] = got[rows, :]


def assemble(core, out0, out1, got, shape):
    return pl.pallas_call(
        assemble_body,
        out_shape=jax.ShapeDtypeStruct(shape, bf16),
        in_specs=[pl.BlockSpec(memory_space=SMEM)] + [pl.BlockSpec(memory_space=VMEM)] * 3,
        out_specs=pl.BlockSpec(memory_space=VMEM),
        compiler_params=params(6),
        name="assemble",
    )(core, out0, out1, got)


HOLD = 1950
AHEAD = 2
RESIDENT = False
LONG = 1 << 35


def shards(tokens, expert_ids, gate_weights, norm_gain, w_gate, w_up, w_down):
    micro, tok_dev, width = tokens.shape
    top = expert_ids.shape[-1]
    groups = lax.axis_size("expert")
    half = width // 2
    cap = 2 * tok_dev * top // groups
    slots = groups * 2 * cap
    core = lax.axis_index("segment")
    swap = lambda value: lax.ppermute(value, "segment", SWAP)

    def travel(rows):
        boxes = rows.reshape(groups, 2 * cap, half)
        return lax.all_to_all(
            boxes, "expert", split_axis=0, concat_axis=0, tiled=True
        ).reshape(slots, half)

    ids = expert_ids[0].transpose(0, 2, 1)
    gates = gate_weights[0].transpose(0, 2, 1)
    ids_other, gates_other, gain_other = swap(ids), swap(gates), swap(norm_gain)
    local = (w_gate[0, 0], w_up[0, 0], w_down[0, 0])
    *tied, ids_other, gates_other, gain_other = lax.optimization_barrier(
        (*local, ids_other, gates_other, gain_other)
    )
    other = tuple(swap(w) for w in tied)
    pin = lambda value: pltpu.with_memory_space_constraint(value, HBM)
    small = (pin(norm_gain), gain_other, pin(ids), ids_other, pin(gates), gates_other)
    tokens = pin(tokens)
    info = [jnp.stack([core, (core == s).astype(core.dtype)]).astype(jnp.int32) for s in range(2)]
    info = lax.optimization_barrier(info)
    send, comb0 = begin(info[0], tokens, small, slots, half, cap, HOLD)
    y = experts(info[0], travel(send), local, other, cap, False)
    out0, send, comb1 = middle(info[1], travel(y), comb0, tokens, small, cap)
    y = experts(info[1], travel(send), local, other, cap, RESIDENT)
    out1, passed = combine(info[0], travel(y), comb1, out0)
    return assemble(info[0], out0, out1, swap(passed), (micro, tok_dev, width))[None]


def solution(mesh):
    in_specs = (
        P(None, "expert", None),
        P("segment", None, "expert", None),
        P("segment", None, "expert", None),
        P("segment", None),
        P("segment", "expert", None, None),
        P("segment", "expert", None, None),
        P("segment", "expert", None, None),
    )
    out_specs = P("segment", None, "expert", None)
    return jax.shard_map(shards, mesh=mesh, in_specs=in_specs, out_specs=out_specs, check_vma=False)
```

```python
import functools

import jax
import jax.numpy as jnp
from jax import lax
from jax.experimental import pallas as pl
from jax.experimental.pallas import tpu as pltpu
from jax.sharding import PartitionSpec as P

VMEM = pltpu.MemorySpace.VMEM
SMEM = pltpu.MemorySpace.SMEM
HBM = pltpu.MemorySpace.HBM
SWAP = [(0, 1), (1, 0)]
SMALL_IN = [HBM, HBM, pl.ANY, HBM, pl.ANY, HBM, pl.ANY]
bf16, f32 = jnp.bfloat16, jnp.float32


def params(mib):
    return pltpu.CompilerParams(vmem_limit_bytes=mib << 20)


def cost(flops, moved):
    return pl.CostEstimate(flops=flops, bytes_accessed=moved, transcendentals=0)


def fetch_small(core_ref, section_sources, scratch, sems):
    core = core_ref[0]
    local = core_ref[1] == 1
    mine, theirs = section_sources[0::2], section_sources[1::2]

    def jobs(sources):
        picked = [sources[0], sources[1].at[core], sources[2].at[core]]
        return [
            pltpu.make_async_copy(source, target, sems.at[k])
            for k, (source, target) in enumerate(zip(picked, scratch))
        ]

    @pl.when(local)
    def _():
        for job in jobs(mine):
            job.start()

    @pl.when(jnp.logical_not(local))
    def _():
        for job in jobs(theirs):
            job.start()

    return jobs(mine)


def route(cap, ids, gates, slots):
    ids = ids.astype(f32).T
    gates = gates.T
    tok, top = ids.shape
    rows = 2 * tok
    ids = jnp.concatenate([ids, ids], axis=0)
    gates = jnp.concatenate([gates, gates], axis=0)
    lane = lax.broadcasted_iota(jnp.int32, (rows, slots), 1)
    row = lax.broadcasted_iota(jnp.int32, (rows, slots), 0)
    expert = lax.div(lane, 2 * cap).astype(f32)
    rank_of = lax.rem(lane, cap).astype(f32)
    same = lax.rem(lax.div(lane, cap), 2) == lax.div(row, tok)
    named = jnp.zeros((rows, slots), f32)
    weight = jnp.zeros((rows, slots), f32)
    for k in range(top):
        hit = ids[:, k : k + 1] == expert
        named += jnp.where(hit, 1.0, 0.0)
        weight += jnp.where(hit, gates[:, k : k + 1], 0.0)
    a = lax.broadcasted_iota(jnp.int32, (rows, rows), 0)
    b = lax.broadcasted_iota(jnp.int32, (rows, rows), 1)
    before = jnp.where((b < a) & (lax.div(a, tok) == lax.div(b, tok)), 1.0, 0.0)
    rank = jnp.dot(before.astype(bf16), named.astype(bf16), preferred_element_type=f32)
    chosen = jnp.where(same & (named > 0.0) & (rank == rank_of), 1.0, 0.0)
    return chosen, chosen * weight


def put_mix(mix, comb_ref):
    rows = mix.shape[0]
    high = mix.astype(bf16)
    comb_ref[0:rows, :] = high
    comb_ref[rows : 2 * rows, :] = (mix - high.astype(f32)).astype(bf16)


def put_rows(x, gain, picker, send_ref):
    rows, half = x.shape
    tok = rows // 2
    squares = jnp.sum(x * x, axis=-1, keepdims=True)
    scale = lax.rsqrt((squares[0:tok] + squares[tok:rows]) / (2 * half) + 1e-06)
    n0 = x[0:tok] * scale * gain[:, 0:half]
    n1 = x[tok:rows] * scale * gain[:, half : 2 * half]
    normed = jnp.concatenate([n0, n1], axis=0).astype(bf16)
    step = 256
    for at in range(0, half, step):
        send_ref[:, at : at + step] = jnp.dot(
            picker, normed[:, at : at + step], preferred_element_type=f32
        ).astype(bf16)


def stacked(x):
    half = x.shape[1] // 2
    return jnp.concatenate([x[:, 0:half], x[:, half : 2 * half]], axis=0).astype(f32)


def begin_body(
    cap, hold, core_ref, tokens, n0, n1, i0, i1, w0, w1, send_ref, comb_ref, pick1_ref, comb1_ref,
    x_s, gain_s, ids_s, gw_s, gain_t, ids_t, gw_t, spun, sems, sems_t
):
    core = core_ref[0]
    small = (n0, n1, i0, i1, w0, w1)
    jobs = [pltpu.make_async_copy(tokens.at[core], x_s, sems.at[3])]
    jobs[0].start()
    jobs += fetch_small(core_ref, small, (gain_s, ids_s, gw_s), sems)
    jobs += fetch_small((core, 1 - core_ref[1]), small, (gain_t, ids_t, gw_t), sems_t)
    spun[...] = jnp.full(spun.shape, 0.5, f32)

    def turn(_, carry):
        spun[...] = spun[...] * 0.5 + 0.25
        return carry

    lax.fori_loop(0, core * hold, turn, 0)
    for job in jobs:
        job.wait()
    chosen, mix = route(cap, ids_s[...], gw_s[...], send_ref.shape[0])
    put_mix(mix, comb_ref)
    put_rows(stacked(x_s[...]), gain_s[...], chosen.T.astype(bf16), send_ref)
    chosen, mix = route(cap, ids_t[...], gw_t[...], send_ref.shape[0])
    put_mix(mix, comb1_ref)
    pick1_ref[...] = chosen.T.astype(bf16)


def begin(core, tokens, small, slots, half, cap, hold):
    tok, width = tokens.shape[1:]
    top = small[2].shape[1]
    section = [
        pltpu.VMEM((1, width), f32),
        pltpu.VMEM((top, tok), jnp.int32),
        pltpu.VMEM((top, tok), f32),
    ]
    mix = jax.ShapeDtypeStruct((4 * tok, slots), bf16)
    return pl.pallas_call(
        functools.partial(begin_body, cap, hold),
        out_shape=(
            jax.ShapeDtypeStruct((slots, half), bf16),
            mix,
            jax.ShapeDtypeStruct((slots, 2 * tok), bf16),
            mix,
        ),
        in_specs=[pl.BlockSpec(memory_space=SMEM)]
        + [pl.BlockSpec(memory_space=m) for m in SMALL_IN],
        out_specs=(pl.BlockSpec(memory_space=VMEM),) * 4,
        scratch_shapes=[
            pltpu.VMEM((tok, width), bf16),
            *section,
            *section,
            pltpu.VMEM((8, 128), f32),
            pltpu.SemaphoreType.DMA((4,)),
            pltpu.SemaphoreType.DMA((4,)),
        ],
        compiler_params=params(8),
        cost_estimate=cost(LONG, 2 * slots * half),
        name="begin",
    )(core, tokens, *small)


def mixed(y_ref, comb_ref):
    both = jnp.dot(comb_ref[...], y_ref[...], preferred_element_type=f32)
    rows = both.shape[0] // 2
    return both[0:rows] + both[rows : 2 * rows]


def middle_body(core_ref, y_ref, old_ref, pick_ref, tokens, n0, n1, x_ref, send_ref, x_s, gain_s, sems):
    core = core_ref[0]
    local = core_ref[1] == 1
    jobs = [
        pltpu.make_async_copy(tokens.at[core], x_s, sems.at[0]),
        pltpu.make_async_copy(n0, gain_s, sems.at[1]),
    ]
    jobs[0].start()

    @pl.when(local)
    def _():
        jobs[1].start()

    @pl.when(jnp.logical_not(local))
    def _():
        pltpu.make_async_copy(n1, gain_s, sems.at[1]).start()

    added = mixed(y_ref, old_ref)
    for job in jobs:
        job.wait()
    x = (stacked(x_s[...]) + added).astype(bf16)
    x_ref[...] = x
    put_rows(x.astype(f32), gain_s[...], pick_ref[...], send_ref)


def middle(core, y, old, pick, tokens, small):
    slots, half = y.shape
    tok, width = tokens.shape[1:]
    return pl.pallas_call(
        middle_body,
        out_shape=(
            jax.ShapeDtypeStruct((2 * tok, half), bf16),
            jax.ShapeDtypeStruct((slots, half), bf16),
        ),
        in_specs=[pl.BlockSpec(memory_space=SMEM)]
        + [pl.BlockSpec(memory_space=VMEM)] * 3
        + [pl.BlockSpec(memory_space=m) for m in SMALL_IN[0:3]],
        out_specs=(pl.BlockSpec(memory_space=VMEM),) * 2,
        scratch_shapes=[
            pltpu.VMEM((tok, width), bf16),
            pltpu.VMEM((1, width), f32),
            pltpu.SemaphoreType.DMA((2,)),
        ],
        compiler_params=params(8),
        cost_estimate=cost(LONG, 4 * slots * half),
        name="middle",
    )(core, y, old, pick, tokens, *small[0:2])


def placing(size, cap, back):
    wide = lax.broadcasted_iota(jnp.int32, (size, size), 1 if back else 0)
    tall = lax.broadcasted_iota(jnp.int32, (size, size), 0 if back else 1)
    part = lax.div(wide, size // 2)
    at = lax.rem(wide, size // 2)
    home = lax.div(at, cap) * (2 * cap) + part * cap + lax.rem(at, cap)
    return jnp.where(home == tall, 1.0, 0.0).astype(bf16)


def experts_body(cap, tiles, ahead, resident, core_ref, x_ref, g0, u0, d0, g1, u1, d1, o_ref, xs, hs, sems, *streams):
    slots, half = x_ref.shape
    wide = hs.shape[1]
    up_tile = wide // tiles
    down_tile = half // tiles_down(half)
    steps = tiles + tiles_down(half)
    group = 256
    local = core_ref[1] == 1

    def copies(step):
        wg, wu, wd = streams
        if step < tiles:
            cols = [pl.ds(step * up_tile, up_tile)] * 2
            pairs = [(g1, wg), (u1, wu)]
        else:
            at = (step - tiles) * down_tile
            cols = [pl.ds(at, down_tile), pl.ds(half + at, down_tile)]
            pairs = [(d1, wd)] * 2
        return [
            pltpu.make_async_copy(source.at[:, c], target.at[:, c], sems.at[2 * step + k])
            for k, (c, (source, target)) in enumerate(zip(cols, pairs))
        ]

    def start(step):
        if step < steps:
            for job in copies(step):
                job.start()

    def wait(step):
        for job in copies(step):
            job.wait()

    if not resident:

        @pl.when(jnp.logical_not(local))
        def _():
            for step in range(ahead):
                start(step)

    place = placing(group, cap, False)
    back = placing(group, cap, True)
    for at in range(0, slots, group):
        for col in range(0, half, 512):
            rows = jnp.dot(
                place, x_ref[at : at + group, col : col + 512], preferred_element_type=f32
            ).astype(bf16)
            xs[at // 2 : at // 2 + group // 2, col : col + 512] = rows[0 : group // 2]
            xs[at // 2 : at // 2 + group // 2, half + col : half + col + 512] = rows[group // 2 :]

    def run(g, u, d, fetched):
        for t in range(tiles):
            if fetched:
                wait(t)
                start(t + ahead)
            cols = pl.ds(t * up_tile, up_tile)
            gate = jnp.dot(xs[...], g[:, cols], preferred_element_type=f32)
            up = jnp.dot(xs[...], u[:, cols], preferred_element_type=f32)
            hs[:, cols] = (jax.nn.silu(gate) * up).astype(bf16)
        for t in range(steps - tiles):
            if fetched:
                wait(tiles + t)
                start(tiles + t + ahead)
            cols = pl.ds(t * down_tile, down_tile)
            parts = [
                jnp.dot(
                    hs[...],
                    d[:, pl.ds(h * half + t * down_tile, down_tile)],
                    preferred_element_type=f32,
                ).astype(bf16)
                for h in range(2)
            ]
            for at in range(0, slots, group):
                pair = jnp.concatenate([p[at // 2 : at // 2 + group // 2] for p in parts], axis=0)
                o_ref[at : at + group, cols] = jnp.dot(
                    back, pair, preferred_element_type=f32
                ).astype(bf16)

    @pl.when(local)
    def _():
        run(g0, u0, d0, False)

    @pl.when(jnp.logical_not(local))
    def _():
        run(*((g1, u1, d1) if resident else streams), not resident)


def tiles_down(half):
    return half // 512


def experts(core, x, local, other, cap, resident):
    slots, half = x.shape
    wide = local[0].shape[1]
    tiles = 3
    rows = slots // 2
    flops = 6 * rows * 2 * half * wide
    if not resident:
        other = tuple(pltpu.with_memory_space_constraint(w, HBM) for w in other)
    return pl.pallas_call(
        functools.partial(experts_body, cap, tiles, AHEAD, resident),
        out_shape=jax.ShapeDtypeStruct((slots, half), bf16),
        in_specs=[pl.BlockSpec(memory_space=SMEM)]
        + [pl.BlockSpec(memory_space=VMEM)] * 4
        + [pl.BlockSpec(memory_space=VMEM if resident else pl.ANY)] * 3,
        out_specs=pl.BlockSpec(memory_space=VMEM),
        scratch_shapes=[
            pltpu.VMEM((rows, 2 * half), bf16),
            pltpu.VMEM((rows, wide), bf16),
            pltpu.SemaphoreType.DMA((2 * tiles + 2 * tiles_down(half),)),
        ]
        + ([] if resident else [pltpu.VMEM(w.shape, bf16) for w in other]),
        compiler_params=params(7 if resident else 26),
        cost_estimate=cost(flops, 6 * half * wide * 2),
        name="experts",
    )(core, x, *local, *other)


def combine_body(core_ref, y_ref, comb_ref, x_ref, out_ref, pass_ref):
    x = x_ref[...]
    out = (x.astype(f32) + mixed(y_ref, comb_ref)).astype(bf16)
    out_ref[...] = out
    pass_ref[...] = jnp.where(core_ref[0] == 0, out, x)


def combine(core, y, comb, x):
    slots, half = y.shape
    return pl.pallas_call(
        combine_body,
        out_shape=(jax.ShapeDtypeStruct(x.shape, bf16),) * 2,
        in_specs=[pl.BlockSpec(memory_space=SMEM)] + [pl.BlockSpec(memory_space=VMEM)] * 3,
        out_specs=(pl.BlockSpec(memory_space=VMEM),) * 2,
        compiler_params=params(6),
        cost_estimate=cost(4 * x.shape[0] * half * slots, 2 * slots * half),
        name="combine",
    )(core, y, comb, x)


def assemble_body(core_ref, out0, out1, got, o_ref):
    core = core_ref[0]
    tok = o_ref.shape[1]
    half = out0.shape[1]
    for h in range(2):
        rows, cols = slice(h * tok, (h + 1) * tok), slice(h * half, (h + 1) * half)
        mine = jnp.where(core == 0, out0[rows, :], out1[rows, :])
        o_ref[core, :, cols] = mine
        o_ref[1 - core, :, cols] = got[rows, :]


def assemble(core, out0, out1, got, shape):
    return pl.pallas_call(
        assemble_body,
        out_shape=jax.ShapeDtypeStruct(shape, bf16),
        in_specs=[pl.BlockSpec(memory_space=SMEM)] + [pl.BlockSpec(memory_space=VMEM)] * 3,
        out_specs=pl.BlockSpec(memory_space=VMEM),
        compiler_params=params(6),
        name="assemble",
    )(core, out0, out1, got)


HOLD = 1900
AHEAD = 3
RESIDENT = False
LONG = 1 << 35


def shards(tokens, expert_ids, gate_weights, norm_gain, w_gate, w_up, w_down):
    micro, tok_dev, width = tokens.shape
    top = expert_ids.shape[-1]
    groups = lax.axis_size("expert")
    half = width // 2
    cap = 2 * tok_dev * top // groups
    slots = groups * 2 * cap
    core = lax.axis_index("segment")
    swap = lambda value: lax.ppermute(value, "segment", SWAP)

    def travel(rows):
        boxes = rows.reshape(groups, 2 * cap, half)
        return lax.all_to_all(
            boxes, "expert", split_axis=0, concat_axis=0, tiled=True
        ).reshape(slots, half)

    ids = expert_ids[0].transpose(0, 2, 1)
    gates = gate_weights[0].transpose(0, 2, 1)
    ids_other, gates_other, gain_other = swap(ids), swap(gates), swap(norm_gain)
    local = (w_gate[0, 0], w_up[0, 0], w_down[0, 0])
    *tied, ids_other, gates_other, gain_other = lax.optimization_barrier(
        (*local, ids_other, gates_other, gain_other)
    )
    other = tuple(swap(w) for w in tied)
    pin = lambda value: pltpu.with_memory_space_constraint(value, HBM)
    small = (pin(norm_gain), gain_other, pin(ids), ids_other, pin(gates), gates_other)
    tokens = pin(tokens)
    info = [jnp.stack([core, (core == s).astype(core.dtype)]).astype(jnp.int32) for s in range(2)]
    info = lax.optimization_barrier(info)
    send, comb0, pick1, comb1 = begin(info[0], tokens, small, slots, half, cap, HOLD)
    y = experts(info[0], travel(send), local, other, cap, False)
    out0, send = middle(info[1], travel(y), comb0, pick1, tokens, small)
    y = experts(info[1], travel(send), local, other, cap, RESIDENT)
    out1, passed = combine(info[0], travel(y), comb1, out0)
    return assemble(info[0], out0, out1, swap(passed), (micro, tok_dev, width))[None]


def solution(mesh):
    in_specs = (
        P(None, "expert", None),
        P("segment", None, "expert", None),
        P("segment", None, "expert", None),
        P("segment", None),
        P("segment", "expert", None, None),
        P("segment", "expert", None, None),
        P("segment", "expert", None, None),
    )
    out_specs = P("segment", None, "expert", None)
    return jax.shard_map(shards, mesh=mesh, in_specs=in_specs, out_specs=out_specs, check_vma=False)
```

```python
import functools

import jax
import jax.numpy as jnp
from jax import lax
from jax.experimental import pallas as pl
from jax.experimental.pallas import tpu as pltpu
from jax.sharding import PartitionSpec as P

VMEM = pltpu.MemorySpace.VMEM
SMEM = pltpu.MemorySpace.SMEM
HBM = pltpu.MemorySpace.HBM
SWAP = [(0, 1), (1, 0)]
SMALL_IN = [HBM, HBM, pl.ANY, HBM, pl.ANY, HBM, pl.ANY]
bf16, f32 = jnp.bfloat16, jnp.float32


def params(mib):
    return pltpu.CompilerParams(vmem_limit_bytes=mib << 20)


def cost(flops, moved):
    return pl.CostEstimate(flops=flops, bytes_accessed=moved, transcendentals=0)


def fetch_small(core_ref, section_sources, scratch, sems):
    core = core_ref[0]
    local = core_ref[1] == 1
    mine, theirs = section_sources[0::2], section_sources[1::2]

    def jobs(sources):
        picked = [sources[0], sources[1].at[core], sources[2].at[core]]
        return [
            pltpu.make_async_copy(source, target, sems.at[k])
            for k, (source, target) in enumerate(zip(picked, scratch))
        ]

    @pl.when(local)
    def _():
        for job in jobs(mine):
            job.start()

    @pl.when(jnp.logical_not(local))
    def _():
        for job in jobs(theirs):
            job.start()

    return jobs(mine)


def route(cap, ids, gates, slots):
    ids = ids.astype(f32).T
    gates = gates.T
    tok, top = ids.shape
    rows = 2 * tok
    ids = jnp.concatenate([ids, ids], axis=0)
    gates = jnp.concatenate([gates, gates], axis=0)
    lane = lax.broadcasted_iota(jnp.int32, (rows, slots), 1)
    row = lax.broadcasted_iota(jnp.int32, (rows, slots), 0)
    expert = lax.div(lane, 2 * cap).astype(f32)
    rank_of = lax.rem(lane, cap).astype(f32)
    same = lax.rem(lax.div(lane, cap), 2) == lax.div(row, tok)
    named = jnp.zeros((rows, slots), f32)
    weight = jnp.zeros((rows, slots), f32)
    for k in range(top):
        hit = ids[:, k : k + 1] == expert
        named += jnp.where(hit, 1.0, 0.0)
        weight += jnp.where(hit, gates[:, k : k + 1], 0.0)
    a = lax.broadcasted_iota(jnp.int32, (rows, rows), 0)
    b = lax.broadcasted_iota(jnp.int32, (rows, rows), 1)
    before = jnp.where((b < a) & (lax.div(a, tok) == lax.div(b, tok)), 1.0, 0.0)
    rank = jnp.dot(before.astype(bf16), named.astype(bf16), preferred_element_type=f32)
    chosen = jnp.where(same & (named > 0.0) & (rank == rank_of), 1.0, 0.0)
    return chosen, chosen * weight


def put_rows(x, gain, chosen, mix, send_ref, comb_ref):
    rows, half = x.shape
    tok = rows // 2
    high = mix.astype(bf16)
    comb_ref[0:rows, :] = high
    comb_ref[rows : 2 * rows, :] = (mix - high.astype(f32)).astype(bf16)
    squares = jnp.sum(x * x, axis=-1, keepdims=True)
    scale = lax.rsqrt((squares[0:tok] + squares[tok:rows]) / (2 * half) + 1e-06)
    n0 = x[0:tok] * scale * gain[:, 0:half]
    n1 = x[tok:rows] * scale * gain[:, half : 2 * half]
    normed = jnp.concatenate([n0, n1], axis=0).astype(bf16)
    picker = chosen.T.astype(bf16)
    step = 256
    for at in range(0, half, step):
        send_ref[:, at : at + step] = jnp.dot(
            picker, normed[:, at : at + step], preferred_element_type=f32
        ).astype(bf16)


def stacked(x):
    half = x.shape[1] // 2
    return jnp.concatenate([x[:, 0:half], x[:, half : 2 * half]], axis=0).astype(f32)


def begin_body(
    cap, hold, core_ref, tokens, n0, n1, i0, i1, w0, w1, send_ref, comb_ref, x_s, gain_s, ids_s, gw_s, spun, sems
):
    core = core_ref[0]
    jobs = [pltpu.make_async_copy(tokens.at[core], x_s, sems.at[3])]
    jobs[0].start()
    jobs += fetch_small(core_ref, (n0, n1, i0, i1, w0, w1), (gain_s, ids_s, gw_s), sems)
    spun[...] = jnp.full(spun.shape, 0.5, f32)

    def turn(_, carry):
        spun[...] = spun[...] * 0.5 + 0.25
        return carry

    lax.fori_loop(0, core * hold, turn, 0)
    for job in jobs:
        job.wait()
    chosen, mix = route(cap, ids_s[...], gw_s[...], send_ref.shape[0])
    put_rows(stacked(x_s[...]), gain_s[...], chosen, mix, send_ref, comb_ref)


def begin(core, tokens, small, slots, half, cap, hold):
    tok, width = tokens.shape[1:]
    top = small[2].shape[1]
    return pl.pallas_call(
        functools.partial(begin_body, cap, hold),
        out_shape=(
            jax.ShapeDtypeStruct((slots, half), bf16),
            jax.ShapeDtypeStruct((4 * tok, slots), bf16),
        ),
        in_specs=[pl.BlockSpec(memory_space=SMEM)]
        + [pl.BlockSpec(memory_space=m) for m in SMALL_IN],
        out_specs=(pl.BlockSpec(memory_space=VMEM),) * 2,
        scratch_shapes=[
            pltpu.VMEM((tok, width), bf16),
            pltpu.VMEM((1, width), f32),
            pltpu.VMEM((top, tok), jnp.int32),
            pltpu.VMEM((top, tok), f32),
            pltpu.VMEM((8, 128), f32),
            pltpu.SemaphoreType.DMA((4,)),
        ],
        compiler_params=params(8),
        cost_estimate=cost(LONG, 2 * slots * half),
        name="begin",
    )(core, tokens, *small)


def mixed(y_ref, comb_ref):
    both = jnp.dot(comb_ref[...], y_ref[...], preferred_element_type=f32)
    rows = both.shape[0] // 2
    return both[0:rows] + both[rows : 2 * rows]


def middle_body(
    cap, core_ref, y_ref, old_ref, tokens, n0, n1, i0, i1, w0, w1, x_ref, send_ref, comb_ref, x_s, gain_s, ids_s, gw_s, sems
):
    jobs = [pltpu.make_async_copy(tokens.at[core_ref[0]], x_s, sems.at[3])]
    jobs[0].start()
    jobs += fetch_small(core_ref, (n0, n1, i0, i1, w0, w1), (gain_s, ids_s, gw_s), sems)
    added = mixed(y_ref, old_ref)
    for job in jobs:
        job.wait()
    chosen, mix = route(cap, ids_s[...], gw_s[...], send_ref.shape[0])
    x = (stacked(x_s[...]) + added).astype(bf16)
    x_ref[...] = x
    put_rows(x.astype(f32), gain_s[...], chosen, mix, send_ref, comb_ref)


def middle(core, y, old, tokens, small, cap):
    slots, half = y.shape
    tok, width = tokens.shape[1:]
    top = small[2].shape[1]
    return pl.pallas_call(
        functools.partial(middle_body, cap),
        out_shape=(
            jax.ShapeDtypeStruct((2 * tok, half), bf16),
            jax.ShapeDtypeStruct((slots, half), bf16),
            jax.ShapeDtypeStruct((4 * tok, slots), bf16),
        ),
        in_specs=[pl.BlockSpec(memory_space=SMEM)]
        + [pl.BlockSpec(memory_space=VMEM)] * 2
        + [pl.BlockSpec(memory_space=m) for m in SMALL_IN],
        out_specs=(pl.BlockSpec(memory_space=VMEM),) * 3,
        scratch_shapes=[
            pltpu.VMEM((tok, width), bf16),
            pltpu.VMEM((1, width), f32),
            pltpu.VMEM((top, tok), jnp.int32),
            pltpu.VMEM((top, tok), f32),
            pltpu.SemaphoreType.DMA((4,)),
        ],
        compiler_params=params(8),
        cost_estimate=cost(LONG, 4 * slots * half),
        name="middle",
    )(core, y, old, tokens, *small)


def placing(size, cap, back):
    wide = lax.broadcasted_iota(jnp.int32, (size, size), 1 if back else 0)
    tall = lax.broadcasted_iota(jnp.int32, (size, size), 0 if back else 1)
    part = lax.div(wide, size // 2)
    at = lax.rem(wide, size // 2)
    home = lax.div(at, cap) * (2 * cap) + part * cap + lax.rem(at, cap)
    return jnp.where(home == tall, 1.0, 0.0).astype(bf16)


def experts_body(cap, tiles, ahead, resident, core_ref, x_ref, g0, u0, d0, g1, u1, d1, o_ref, xs, hs, sems, *streams):
    slots, half = x_ref.shape
    wide = hs.shape[1]
    up_tile = wide // tiles
    down_tile = half // tiles_down(half)
    steps = tiles + tiles_down(half)
    group = 256
    local = core_ref[1] == 1

    def copies(step):
        wg, wu, wd = streams
        if step < tiles:
            cols = [pl.ds(step * up_tile, up_tile)] * 2
            pairs = [(g1, wg), (u1, wu)]
        else:
            at = (step - tiles) * down_tile
            cols = [pl.ds(at, down_tile), pl.ds(half + at, down_tile)]
            pairs = [(d1, wd)] * 2
        return [
            pltpu.make_async_copy(source.at[:, c], target.at[:, c], sems.at[2 * step + k])
            for k, (c, (source, target)) in enumerate(zip(cols, pairs))
        ]

    def start(step):
        if step < steps:
            for job in copies(step):
                job.start()

    def wait(step):
        for job in copies(step):
            job.wait()

    if not resident:

        @pl.when(jnp.logical_not(local))
        def _():
            for step in range(ahead):
                start(step)

    place = placing(group, cap, False)
    back = placing(group, cap, True)
    for at in range(0, slots, group):
        for col in range(0, half, 512):
            rows = jnp.dot(
                place, x_ref[at : at + group, col : col + 512], preferred_element_type=f32
            ).astype(bf16)
            xs[at // 2 : at // 2 + group // 2, col : col + 512] = rows[0 : group // 2]
            xs[at // 2 : at // 2 + group // 2, half + col : half + col + 512] = rows[group // 2 :]

    def run(g, u, d, fetched):
        for t in range(tiles):
            if fetched:
                wait(t)
                start(t + ahead)
            cols = pl.ds(t * up_tile, up_tile)
            gate = jnp.dot(xs[...], g[:, cols], preferred_element_type=f32)
            up = jnp.dot(xs[...], u[:, cols], preferred_element_type=f32)
            hs[:, cols] = (jax.nn.silu(gate) * up).astype(bf16)
        for t in range(steps - tiles):
            if fetched:
                wait(tiles + t)
                start(tiles + t + ahead)
            cols = pl.ds(t * down_tile, down_tile)
            parts = [
                jnp.dot(
                    hs[...],
                    d[:, pl.ds(h * half + t * down_tile, down_tile)],
                    preferred_element_type=f32,
                ).astype(bf16)
                for h in range(2)
            ]
            for at in range(0, slots, group):
                pair = jnp.concatenate([p[at // 2 : at // 2 + group // 2] for p in parts], axis=0)
                o_ref[at : at + group, cols] = jnp.dot(
                    back, pair, preferred_element_type=f32
                ).astype(bf16)

    @pl.when(local)
    def _():
        run(g0, u0, d0, False)

    @pl.when(jnp.logical_not(local))
    def _():
        run(*((g1, u1, d1) if resident else streams), not resident)


def tiles_down(half):
    return half // 1024


def experts(core, x, local, other, cap, resident):
    slots, half = x.shape
    wide = local[0].shape[1]
    tiles = 3
    rows = slots // 2
    flops = 6 * rows * 2 * half * wide
    if not resident:
        other = tuple(pltpu.with_memory_space_constraint(w, HBM) for w in other)
    return pl.pallas_call(
        functools.partial(experts_body, cap, tiles, AHEAD, resident),
        out_shape=jax.ShapeDtypeStruct((slots, half), bf16),
        in_specs=[pl.BlockSpec(memory_space=SMEM)]
        + [pl.BlockSpec(memory_space=VMEM)] * 4
        + [pl.BlockSpec(memory_space=VMEM if resident else pl.ANY)] * 3,
        out_specs=pl.BlockSpec(memory_space=VMEM),
        scratch_shapes=[
            pltpu.VMEM((rows, 2 * half), bf16),
            pltpu.VMEM((rows, wide), bf16),
            pltpu.SemaphoreType.DMA((2 * tiles + 2 * tiles_down(half),)),
        ]
        + ([] if resident else [pltpu.VMEM(w.shape, bf16) for w in other]),
        compiler_params=params(7 if resident else 26),
        cost_estimate=cost(flops, 6 * half * wide * 2),
        name="experts",
    )(core, x, *local, *other)


def combine_body(core_ref, y_ref, comb_ref, x_ref, out_ref, pass_ref):
    x = x_ref[...]
    out = (x.astype(f32) + mixed(y_ref, comb_ref)).astype(bf16)
    out_ref[...] = out
    pass_ref[...] = jnp.where(core_ref[0] == 0, out, x)


def combine(core, y, comb, x):
    slots, half = y.shape
    return pl.pallas_call(
        combine_body,
        out_shape=(jax.ShapeDtypeStruct(x.shape, bf16),) * 2,
        in_specs=[pl.BlockSpec(memory_space=SMEM)] + [pl.BlockSpec(memory_space=VMEM)] * 3,
        out_specs=(pl.BlockSpec(memory_space=VMEM),) * 2,
        compiler_params=params(6),
        cost_estimate=cost(4 * x.shape[0] * half * slots, 2 * slots * half),
        name="combine",
    )(core, y, comb, x)


def assemble_body(core_ref, out0, out1, got, o_ref):
    core = core_ref[0]
    tok = o_ref.shape[1]
    half = out0.shape[1]
    for h in range(2):
        rows, cols = slice(h * tok, (h + 1) * tok), slice(h * half, (h + 1) * half)
        mine = jnp.where(core == 0, out0[rows, :], out1[rows, :])
        o_ref[core, :, cols] = mine
        o_ref[1 - core, :, cols] = got[rows, :]


def assemble(core, out0, out1, got, shape):
    return pl.pallas_call(
        assemble_body,
        out_shape=jax.ShapeDtypeStruct(shape, bf16),
        in_specs=[pl.BlockSpec(memory_space=SMEM)] + [pl.BlockSpec(memory_space=VMEM)] * 3,
        out_specs=pl.BlockSpec(memory_space=VMEM),
        compiler_params=params(6),
        name="assemble",
    )(core, out0, out1, got)


HOLD = 1950
AHEAD = 2
RESIDENT = False
LONG = 1 << 35


def shards(tokens, expert_ids, gate_weights, norm_gain, w_gate, w_up, w_down):
    micro, tok_dev, width = tokens.shape
    top = expert_ids.shape[-1]
    groups = lax.axis_size("expert")
    half = width // 2
    cap = 2 * tok_dev * top // groups
    slots = groups * 2 * cap
    core = lax.axis_index("segment")
    swap = lambda value: lax.ppermute(value, "segment", SWAP)

    def travel(rows):
        boxes = rows.reshape(groups, 2 * cap, half)
        return lax.all_to_all(
            boxes, "expert", split_axis=0, concat_axis=0, tiled=True
        ).reshape(slots, half)

    ids = expert_ids[0].transpose(0, 2, 1)
    gates = gate_weights[0].transpose(0, 2, 1)
    ids_other, gates_other, gain_other = swap(ids), swap(gates), swap(norm_gain)
    local = (w_gate[0, 0], w_up[0, 0], w_down[0, 0])
    *tied, ids_other, gates_other, gain_other = lax.optimization_barrier(
        (*local, ids_other, gates_other, gain_other)
    )
    other = tuple(swap(w) for w in tied)
    pin = lambda value: pltpu.with_memory_space_constraint(value, HBM)
    small = (pin(norm_gain), gain_other, pin(ids), ids_other, pin(gates), gates_other)
    tokens = pin(tokens)
    info = [jnp.stack([core, (core == s).astype(core.dtype)]).astype(jnp.int32) for s in range(2)]
    info = lax.optimization_barrier(info)
    send, comb0 = begin(info[0], tokens, small, slots, half, cap, HOLD)
    y = experts(info[0], travel(send), local, other, cap, False)
    out0, send, comb1 = middle(info[1], travel(y), comb0, tokens, small, cap)
    y = experts(info[1], travel(send), local, other, cap, RESIDENT)
    out1, passed = combine(info[0], travel(y), comb1, out0)
    return assemble(info[0], out0, out1, swap(passed), (micro, tok_dev, width))[None]


def solution(mesh):
    in_specs = (
        P(None, "expert", None),
        P("segment", None, "expert", None),
        P("segment", None, "expert", None),
        P("segment", None),
        P("segment", "expert", None, None),
        P("segment", "expert", None, None),
        P("segment", "expert", None, None),
    )
    out_specs = P("segment", None, "expert", None)
    return jax.shard_map(shards, mesh=mesh, in_specs=in_specs, out_specs=out_specs, check_vma=False)
```
